32 devices in a mesh: wide: 8 (over z, y), narrow: 4 (over x, core).
Axes of the slice: x: 2, y: 2, z: 4, core: 2. Of those that a mesh axis runs over, the one named last changes fastest.
Arguments:
- coefficients: bfloat16 [100, 131072], P(None, ('wide', 'narrow')), may hold values from -6 to 6
- neighbours: int32 [4, 131072], P(None, ('wide', 'narrow')), may hold values from 0 to 5119, as said below
- halo_blocks: int32 [32, 4, 2], P(('wide', 'narrow')), may hold values from 0 to 31, as said below
- recon_weight: bfloat16 [5, 75, 100], replicated, may hold values from -0.25 to 0.25
- owner_device: int32 [1024], P(('wide', 'narrow')), may hold values from 0 to 31, as said below
- work_count: int32 [1024], P(('wide', 'narrow')), may hold values from 1 to 4
Outputs:
- migrated_modal: bfloat16 [100, 131072], P(None, ('wide', 'narrow'))
- migrated_metric: float32 [6, 131072], P(None, ('wide', 'narrow'))
- migrated_work: float32 [131072], P(('wide', 'narrow'))
The draws below stay inside these ranges and needn't reach their ends.
Inputs may be any that keep to these rules, and one draw needn't show every extreme that they name: `neighbours`: A value below 4096 names an element of the same device; a larger one names element i of the h-th block sent to this device from direction k, as in the reference program. `halo_blocks`: each device's list for one direction holds 2 different block numbers of that device. `owner_device`: every device receives exactly 32 blocks. Of one device's blocks, either exactly 4 or none go to devices of any one wide index. Two devices of the same wide index with narrow indices 2j and 2j + 1 together send either exactly 8 or none of their blocks to devices of any one wide index. For every wide index w and narrow indices a and c, exactly 8 of the blocks that devices of narrow index a send to wide index w go to the device of wide index w and narrow index c.
All inputs are finite; a program needn't handle non-finite values.
Results may differ from the reference program's by a relative error of at most 0.0004.
Values may be sent and summed in bfloat16 or wider, within the bound.
No kernel may reach another device: no remote copies, remote signals or barrier semaphores. Data moves between devices by JAX's collectives and lax.ppermute only.
A program may use at most 64 MiB of HBM per device.

```python
from functools import partial
import jax
import jax.numpy as jnp
from jax import lax

BLK = 128
BLOCKS_DEV = 32
COEF = 100
DERIV = 75
HALO_BLOCKS = 2
ELEMS = 131072
BLOCKS = 1024
N_WIDE = 8
N_NARROW = 4
DEVICES = 32


def draw_neighbours(key, part):
    base = jax.random.fold_in(key, 17)
    elems_dev = BLOCKS_DEV * BLK
    halo_size = 4 * HALO_BLOCKS * BLK
    shape_all = (4, DEVICES * elems_dev)
    near = jax.random.randint(jax.random.fold_in(base, 1), shape_all, 0, elems_dev)
    far_ref = jax.random.randint(jax.random.fold_in(base, 2), shape_all, 0, halo_size) + elems_dev
    choose_far = jax.random.randint(jax.random.fold_in(base, 3), shape_all, 0, 5) < 2
    return jnp.where(choose_far, far_ref, near).astype(jnp.int32)


def draw_halo_blocks(key, part):
    base = jax.random.fold_in(key, 23)
    subkeys = jax.random.split(base, DEVICES * 4)
    shuffles = jax.vmap(partial(jax.random.permutation, x=BLOCKS_DEV))(subkeys)
    return shuffles[:, :HALO_BLOCKS].reshape(DEVICES, 4, HALO_BLOCKS).astype(jnp.int32)


def draw_owner_device(key, part):
    base = jax.random.fold_in(key, 31)
    pair_count = N_NARROW // 2
    wide_perm = jax.vmap(partial(jax.random.permutation, x=N_WIDE))(jax.random.split(jax.random.fold_in(base, 1), pair_count))
    wide_start = jax.vmap(partial(jax.random.permutation, x=N_WIDE))(jax.random.split(jax.random.fold_in(base, 2), pair_count))
    labels = jax.vmap(partial(jax.random.permutation, x=BLOCKS_DEV))(jax.random.split(jax.random.fold_in(base, 3), N_WIDE * N_NARROW)) % N_NARROW
    labels = labels.reshape(N_WIDE, N_NARROW, BLOCKS_DEV)
    source_wide = jnp.arange(N_WIDE)[:, None, None]
    source_narrow = jnp.arange(N_NARROW)[None, :, None]
    pair_of = source_narrow // 2
    member = source_narrow % 2
    position = jnp.arange(BLOCKS_DEV)[None, None, :]
    target_wide = wide_perm[pair_of, (wide_start[pair_of, source_wide] + member * BLOCKS_DEV + position) % N_WIDE]
    target_narrow = labels[target_wide, source_narrow, position]
    return (target_wide * N_NARROW + target_narrow).reshape(-1).astype(jnp.int32)


def place_ends(values, key, smallest, largest):
    place = [jax.random.randint(jax.random.fold_in(key, axis), (), 0, length) for axis, length in enumerate(values.shape)]
    main_axis = values.shape.index(max(values.shape))
    next_to = place[:main_axis] + [(place[main_axis] + 1) % values.shape[main_axis]] + place[main_axis + 1:]
    return values.at[tuple(place)].set(smallest).at[tuple(next_to)].set(largest)


def block_levels(stream_key, dims, cuts, low, largest):
    def one(dim, blocks):
        heights = jax.random.uniform(jax.random.fold_in(jax.random.fold_in(stream_key, 6), dim), (blocks,), jnp.float32, low / len(cuts), largest / len(cuts))
        return jnp.repeat(jnp.exp(heights), dims[dim] // blocks).reshape((-1,) + (1,) * (len(dims) - dim - 1))

    loudness = one(*cuts[0])
    for cut in cuts[1:]:
        loudness = loudness * one(*cut)
    return loudness


def bell_draw(own_key, extent, spread, bound, cuts=(), kind=jnp.bfloat16):
    drawn = jax.random.normal(own_key, extent, jnp.float32) * spread
    if len(cuts) > 0:
        drawn = block_levels(own_key, extent, cuts, -0.22, 0.18) * drawn
    return jnp.clip(drawn, min=-bound, max=bound).astype(kind)


def setup_inputs(seed: int = 0) -> dict:
    key_list = jax.random.split(jax.random.key(seed), 7)
    coefficients = bell_draw(key_list[0], (COEF, ELEMS), 1.0, 6.0, ((1, 32),))
    neighbours = draw_neighbours(jax.random.fold_in(key_list[6], 71), 0)
    halo_blocks = draw_halo_blocks(jax.random.fold_in(key_list[6], 71), 0)
    recon_weight = bell_draw(key_list[3], (5, DERIV, COEF), (5 * COEF) ** -0.5, 0.25)
    owner_device = draw_owner_device(jax.random.fold_in(key_list[6], 71), 0)
    work_count = place_ends(jax.random.randint(key_list[5], (BLOCKS,), 1, 5), jax.random.fold_in(key_list[5], 1), 1, 4).astype(jnp.int32)
    return {"coefficients": coefficients, "neighbours": neighbours, "halo_blocks": halo_blocks, "recon_weight": recon_weight, "owner_device": owner_device, "work_count": work_count}


def metric_rows(derivs):
    vectors = derivs.reshape(derivs.shape[0] // 3, 3, derivs.shape[1])
    inverse = 1.0 / vectors.shape[0]
    along_x = vectors[:, 0]
    along_y = vectors[:, 1]
    along_z = vectors[:, 2]
    return jnp.stack([1.0 + inverse * lax.optimization_barrier(jnp.sum(along_x * along_x, axis=0)), 1.0 + inverse * lax.optimization_barrier(jnp.sum(along_y * along_y, axis=0)), 1.0 + inverse * lax.optimization_barrier(jnp.sum(along_z * along_z, axis=0)), inverse * lax.optimization_barrier(jnp.sum(along_x * along_y, axis=0)), inverse * lax.optimization_barrier(jnp.sum(along_x * along_z, axis=0)), inverse * lax.optimization_barrier(jnp.sum(along_y * along_z, axis=0))])

def determinant(components):
    metric_xx = components[0]
    metric_yy = components[1]
    metric_zz = components[2]
    metric_xy = components[3]
    metric_xz = components[4]
    metric_yz = components[5]
    return metric_xx * (metric_yy * metric_zz - metric_yz * metric_yz) - metric_xy * (metric_xy * metric_zz - metric_yz * metric_xz) + metric_xz * (metric_xy * metric_yz - metric_yy * metric_xz)

def reference(coefficients, neighbours, halo_blocks, recon_weight, owner_device, work_count):
    elems_dev = BLOCKS_DEV * BLK
    opposite = jnp.array([1, 0, 3, 2], dtype=jnp.int32)

    def one_device(device):
        wide_at = device // N_NARROW
        narrow_at = device % N_NARROW
        peer_ids = jnp.stack([(wide_at - 1) % N_WIDE * N_NARROW + narrow_at, (wide_at + 1) % N_WIDE * N_NARROW + narrow_at, wide_at * N_NARROW + (narrow_at - 1) % N_NARROW, wide_at * N_NARROW + (narrow_at + 1) % N_NARROW]).astype(jnp.int32)
        first_elem = (device * elems_dev).astype(jnp.int32)
        face_refs = lax.dynamic_slice_in_dim(neighbours, first_elem, elems_dev, 1)
        is_local = face_refs < elems_dev
        offset = jnp.maximum(face_refs - elems_dev, 0)
        slot_index = offset // BLK
        lane_index = offset % BLK
        direction = slot_index // HALO_BLOCKS
        listed = slot_index % HALO_BLOCKS
        sender = peer_ids[direction]
        block_index = halo_blocks[sender, opposite[direction], listed]
        source = jnp.where(is_local, first_elem + face_refs, sender * elems_dev + block_index * BLK + lane_index)
        own_cols = lax.dynamic_slice_in_dim(coefficients, first_elem, elems_dev, 1)
        derivs = jnp.dot(recon_weight[0], own_cols, preferred_element_type=jnp.float32)
        for face_index in range(4):
            gathered = jnp.take(coefficients, source[face_index], axis=1)
            derivs = derivs + jnp.dot(recon_weight[face_index + 1], gathered, preferred_element_type=jnp.float32)
        components = metric_rows(derivs)
        counts = lax.dynamic_slice_in_dim(work_count, (device * BLOCKS_DEV).astype(jnp.int32), BLOCKS_DEV, 0)
        work_est = jnp.repeat(counts.astype(jnp.float32), BLK) * jnp.sqrt(determinant(components))
        return (components, work_est)
    components, work_est = lax.map(one_device, jnp.arange(DEVICES, dtype=jnp.int32))
    metric_all = jnp.transpose(components, (1, 0, 2)).reshape(6, -1)
    work_all = work_est.reshape(-1)
    block_ids = jnp.arange(BLOCKS_DEV * DEVICES, dtype=jnp.int32)
    source_dev = block_ids // BLOCKS_DEV
    sort_key = owner_device * (BLOCKS_DEV * DEVICES) + (source_dev % N_NARROW * N_WIDE + source_dev // N_NARROW) * BLOCKS_DEV + block_ids % BLOCKS_DEV
    ordering = jnp.argsort(sort_key).astype(jnp.int32)

    def regroup(values):
        blocked = values.reshape(values.shape[0], -1, BLK)
        return jnp.take(blocked, ordering, axis=1).reshape(values.shape[0], -1)
    return (regroup(coefficients), regroup(metric_all), regroup(work_all[None, :])[0])
```

```python
import jax
import jax.numpy as jnp
from jax import lax
from jax.experimental import pallas as pl
from jax.experimental.pallas import tpu as pltpu
from jax.sharding import PartitionSpec as P

f32 = jnp.float32
bf16 = jnp.bfloat16
LANES = 128
FACES = 4

SMEM = pl.BlockSpec(memory_space=pltpu.SMEM)
VMEM = pl.BlockSpec(memory_space=pltpu.VMEM)
HBM = pl.BlockSpec(memory_space=pl.ANY)


def passed_along(value, axis, steps):
    count = lax.axis_size(axis)
    pairs = [(source, (source + steps) % count) for source in range(count)]
    return lax.ppermute(value, axis, pairs)


def swapped(value, axis, flip):
    count = lax.axis_size(axis)
    return lax.ppermute(value, axis, [(source, source ^ flip) for source in range(count)])


def padded_rows(rows):
    return (rows // 8 + 1) * 8


def pack_kernel(wide, narrow, coef, halo_blocks, owner, *refs):
    halos, packed, slot, filled = refs[:4], refs[4], refs[5], refs[6]
    rows = coef.shape[0]
    slots, tall = packed.shape[0], packed.shape[1]
    blocks = owner.shape[0]
    per_wide = slots // wide
    for k in range(4):
        for h in range(halo_blocks.shape[2]):
            at = pl.multiple_of(halo_blocks[0, k, h] * LANES, LANES)
            halos[k][h] = coef[:, pl.ds(at, LANES)]

    def clear(w, _):
        filled[w] = 0
        return 0

    lax.fori_loop(0, wide, clear, 0)
    if slots > blocks:
        for t in range(slots):
            packed[t, rows:tall, :] = jnp.full((tall - rows, LANES), -1, bf16)
    for b in range(blocks):
        target = owner[b]
        w = target // narrow
        t = w * per_wide + filled[w]
        filled[w] = filled[w] + 1
        slot[b] = t
        packed[t, 0:rows, :] = coef[:, b * LANES : (b + 1) * LANES]
        packed[t, rows:tall, :] = jnp.full((tall - rows, LANES), (target % narrow).astype(f32)).astype(
            bf16
        )


def pack(coef, halo_blocks, owner, wide, narrow):
    rows, count = coef.shape
    blocks = owner.shape[0]
    slots = wide * max(1, blocks // wide)
    halo = jax.ShapeDtypeStruct((halo_blocks.shape[2], rows, LANES), bf16)
    return pl.pallas_call(
        lambda *refs: pack_kernel(wide, narrow, *refs),
        out_shape=[halo] * 4
        + [
            jax.ShapeDtypeStruct((slots, padded_rows(rows), LANES), bf16),
            jax.ShapeDtypeStruct((blocks,), jnp.int32),
        ],
        in_specs=[VMEM, SMEM, SMEM],
        out_specs=[VMEM] * 5 + [SMEM],
        scratch_shapes=[pltpu.SMEM((wide,), jnp.int32)],
        cost_estimate=pl.CostEstimate(flops=0, bytes_accessed=4 * rows * count, transcendentals=0),
        name="pack",
    )(coef, halo_blocks, owner)


def metric_kernel(nb, slot, count, coef, h0, h1, h2, h3, w, out, y0, y1, y2, y3, acc0, acc1, wp, idx, sem):
    tables = (y0, y1, y2, y3)
    accs = (acc0, acc1)
    rows = w.shape[1]
    third = rows // 3
    elems = coef.shape[1]
    blocks = elems // LANES
    contract = (((1,), (1,)), ((), ()))

    def fetch(b, place):
        at = pl.multiple_of(b * LANES, LANES)
        return pltpu.make_async_copy(nb.at[:, pl.ds(at, LANES)], idx.at[place], sem.at[place])

    fetch(0, 0).start()
    fetch(1, 1).start()
    lane = lax.broadcasted_iota(jnp.int32, (LANES, rows), 0)
    row = lax.broadcasted_iota(jnp.int32, (LANES, rows), 1)
    place = ((row == 3 * (lane % 32) + lane // 32) & (lane % 32 < third)).astype(bf16)
    for f in range(FACES + 1):
        wp[f] = jnp.dot(place, w[f], preferred_element_type=f32).astype(bf16)
    step = 512

    def project(i, _):
        at = pl.multiple_of(i * step, step)
        cols = coef[:, pl.ds(at, step)].T
        for f in range(FACES):
            tables[f][pl.ds(at, step), :] = lax.dot_general(
                cols, wp[f + 1], contract, preferred_element_type=f32
            )
        return 0

    lax.fori_loop(0, elems // step, project, 0)
    for k, halo in enumerate((h0, h1, h2, h3)):
        for h in range(halo.shape[0]):
            cols = halo[h].T
            at = elems + (k * halo.shape[0] + h) * LANES
            for f in range(FACES):
                tables[f][pl.ds(at, LANES), :] = lax.dot_general(
                    cols, wp[f + 1], contract, preferred_element_type=f32
                )

    def gather(place):
        for e in range(LANES):
            part = [tables[f][pl.ds(idx[place, f, e], 1), :] for f in range(FACES)]
            accs[place][pl.ds(e, 1), :] = (part[0] + part[1]) + (part[2] + part[3])

    def metric(b, place):
        at = pl.multiple_of(b * LANES, LANES)
        d = accs[place][...].T + jnp.dot(
            wp[0], coef[:, pl.ds(at, LANES)], preferred_element_type=f32
        )
        x, y, z = d[0:32], d[32:64], d[64:96]
        inverse = 1.0 / third

        def mean(p):
            return inverse * jnp.sum(p, axis=0, keepdims=True)

        xx, yy, zz = 1.0 + mean(x * x), 1.0 + mean(y * y), 1.0 + mean(z * z)
        xy, xz, yz = mean(x * y), mean(x * z), mean(y * z)
        det = xx * (yy * zz - yz * yz) - xy * (xy * zz - yz * xz) + xz * (xy * yz - yy * xz)
        work = count[b].astype(f32) * jnp.sqrt(det)
        out[slot[b]] = jnp.concatenate([xx, yy, zz, xy, xz, yz, work, work], axis=0)

    def pair(i, _):
        b = 2 * i
        fetch(b, 0).wait()
        gather(0)

        @pl.when(i + 1 < blocks // 2)
        def _():
            fetch(b + 2, 0).start()

        fetch(b + 1, 1).wait()
        metric(b, 0)
        gather(1)

        @pl.when(i + 1 < blocks // 2)
        def _():
            fetch(b + 3, 1).start()

        metric(b + 1, 1)
        return 0

    lax.fori_loop(0, blocks // 2, pair, 0)


def metrics(nb, slot, count, coef, halos, w, slots):
    elems = coef.shape[1]
    table = elems + sum(h.shape[0] for h in halos) * LANES
    return pl.pallas_call(
        metric_kernel,
        out_shape=jax.ShapeDtypeStruct((slots, 8, LANES), f32),
        in_specs=[HBM, SMEM, SMEM] + [VMEM] * 6,
        out_specs=VMEM,
        scratch_shapes=[pltpu.VMEM((table, LANES), f32)] * FACES
        + [
            pltpu.VMEM((LANES, LANES), f32),
            pltpu.VMEM((LANES, LANES), f32),
            pltpu.VMEM((FACES + 1, LANES, w.shape[2]), bf16),
            pltpu.SMEM((2, FACES, LANES), jnp.int32),
            pltpu.SemaphoreType.DMA((2,)),
        ],
        cost_estimate=pl.CostEstimate(
            flops=2 * table * 5 * LANES * LANES, bytes_accessed=30 * elems * LANES, transcendentals=elems
        ),
        name="metric",
    )(nb, slot, count, coef, *halos, w)


def relay_kernel(narrow, arrived, *refs):
    sends, order, words, tags, filled, sem = refs[:narrow], *refs[narrow:]
    slots, tall = arrived.shape[0], arrived.shape[1]
    per, rows = sends[0].shape[0], sends[0].shape[1]
    for t in range(slots):
        words[t : t + 1, :] = arrived[t, tall - 8 : tall, :].astype(f32)[7:8].astype(jnp.int32)
    copy = pltpu.make_async_copy(words, tags, sem)
    copy.start()
    copy.wait()
    for c in range(narrow + 1):
        filled[c] = c * per
    for t in range(slots):
        tag = tags[t, 0]
        c = jnp.where(tag < 0, narrow, tag)
        at = filled[c]
        order[at] = t
        filled[c] = at + 1
    mine = lax.axis_index("narrow")
    for k in range(narrow):
        for j in range(per):
            sends[k][j] = arrived[order[(mine ^ k) * per + j], 0:rows, :]


def relay(arrived, rows, narrow, blocks):
    slots = arrived.shape[0]
    per = blocks // narrow
    *sends, order = pl.pallas_call(
        lambda *refs: relay_kernel(narrow, *refs),
        out_shape=[jax.ShapeDtypeStruct((per, rows, LANES), bf16)] * narrow
        + [jax.ShapeDtypeStruct((blocks + slots,), jnp.int32)],
        in_specs=[VMEM],
        out_specs=[VMEM] * narrow + [SMEM],
        scratch_shapes=[
            pltpu.VMEM((slots, LANES), jnp.int32),
            pltpu.SMEM((slots, LANES), jnp.int32),
            pltpu.SMEM((narrow + 1,), jnp.int32),
            pltpu.SemaphoreType.DMA(()),
        ],
        cost_estimate=pl.CostEstimate(
            flops=0, bytes_accessed=4 * blocks * rows * LANES, transcendentals=0
        ),
        name="relay",
    )(arrived)
    return sends, order


def relay_stats_kernel(narrow, arrived, order, *sends):
    per = sends[0].shape[0]
    mine = lax.axis_index("narrow")
    for k in range(narrow):
        for j in range(per):
            sends[k][j] = arrived[order[(mine ^ k) * per + j]]


def relay_stats(arrived, order, narrow, blocks):
    per = blocks // narrow
    return pl.pallas_call(
        lambda *refs: relay_stats_kernel(narrow, *refs),
        out_shape=[jax.ShapeDtypeStruct((per, 8, LANES), f32)] * narrow,
        in_specs=[VMEM, SMEM],
        out_specs=[VMEM] * narrow,
        cost_estimate=pl.CostEstimate(flops=0, bytes_accessed=64 * blocks * LANES, transcendentals=0),
        name="relay_stats",
    )(arrived, order)


def place_kernel(*refs):
    parts, out = refs[:-1], refs[-1]
    per = parts[0].shape[0]
    mine = lax.axis_index("narrow")
    for k, part in enumerate(parts):
        for j in range(per):
            at = pl.multiple_of(((mine ^ k) * per + j) * LANES, LANES)
            out[:, pl.ds(at, LANES)] = part[j]


def place(parts):
    per, rows, _ = parts[0].shape
    return pl.pallas_call(
        place_kernel,
        out_shape=jax.ShapeDtypeStruct((rows, len(parts) * per * LANES), bf16),
        in_specs=[VMEM] * len(parts),
        out_specs=VMEM,
        name="place",
    )(*parts)


def place_stats_kernel(*refs):
    parts, metric, work = refs[:-2], refs[-2], refs[-1]
    per = parts[0].shape[0]
    mine = lax.axis_index("narrow")
    for k, part in enumerate(parts):
        for j in range(per):
            t = (mine ^ k) * per + j
            at = pl.multiple_of(t * LANES, LANES)
            metric[:, pl.ds(at, LANES)] = part[j, 0:6, :]
            work[pl.ds(t, 1), :] = part[j, 6:7, :]


def place_stats(parts):
    per = parts[0].shape[0]
    blocks = len(parts) * per
    return pl.pallas_call(
        place_stats_kernel,
        out_shape=[
            jax.ShapeDtypeStruct((6, blocks * LANES), f32),
            jax.ShapeDtypeStruct((blocks, LANES), f32),
        ],
        in_specs=[VMEM] * len(parts),
        out_specs=[VMEM] * 2,
        name="place_stats",
    )(*parts)


def per_device(coefficients, neighbours, halo_blocks, recon_weight, owner_device, work_count):
    wide = lax.axis_size("wide")
    narrow = lax.axis_size("narrow")
    rows, elems = coefficients.shape
    blocks = owner_device.shape[0]
    to0, to1, to2, to3, packed, slot = pack(coefficients, halo_blocks, owner_device, wide, narrow)
    halos = [
        passed_along(to1, "wide", 1),
        passed_along(to0, "wide", -1),
        passed_along(to3, "narrow", 1),
        passed_along(to2, "narrow", -1),
    ]
    arrived = lax.all_to_all(packed, "wide", 0, 0, tiled=True)
    stats = metrics(
        neighbours, slot, work_count, coefficients, halos, recon_weight, packed.shape[0]
    )
    stats_arrived = lax.all_to_all(stats, "wide", 0, 0, tiled=True)
    sends, order = relay(arrived, rows, narrow, blocks)
    parts = [sends[0]] + [swapped(sends[k], "narrow", k) for k in range(1, narrow)]
    stats_sends = relay_stats(stats_arrived, order, narrow, blocks)
    stats_parts = [stats_sends[0]] + [
        swapped(stats_sends[k], "narrow", k) for k in range(1, narrow)
    ]
    modal = place(parts)
    metric, work = place_stats(stats_parts)
    return modal, metric, work.reshape(-1)


def solution(mesh):
    return jax.shard_map(
        per_device,
        mesh=mesh,
        in_specs=(
            P(None, ("wide", "narrow")),
            P(None, ("wide", "narrow")),
            P(("wide", "narrow"), None, None),
            P(),
            P(("wide", "narrow")),
            P(("wide", "narrow")),
        ),
        out_specs=(P(None, ("wide", "narrow")), P(None, ("wide", "narrow")), P(("wide", "narrow"))),
        check_vma=False,
    )
```

```python
import jax
import jax.numpy as jnp
from jax import lax
from jax.experimental import pallas as pl
from jax.experimental.pallas import tpu as pltpu
from jax.sharding import PartitionSpec as P

f32 = jnp.float32
bf16 = jnp.bfloat16
LANES = 128
FACES = 4
AHEAD = 4

SMEM = pl.BlockSpec(memory_space=pltpu.SMEM)
VMEM = pl.BlockSpec(memory_space=pltpu.VMEM)
HBM = pl.BlockSpec(memory_space=pl.ANY)


def grant(*shapes):
    return pltpu.CompilerParams(vmem_limit_bytes=sum(shapes) + (1 << 20))


def passed_along(value, axis, steps):
    count = lax.axis_size(axis)
    pairs = [(source, (source + steps) % count) for source in range(count)]
    return lax.ppermute(value, axis, pairs)


def swapped(value, axis, flip):
    count = lax.axis_size(axis)
    return lax.ppermute(value, axis, [(source, source ^ flip) for source in range(count)])


def padded_rows(rows):
    return (rows // 8 + 1) * 8


def pack_kernel(wide, narrow, coef, halo_blocks, owner, *refs):
    halos, packed, slot, filled = refs[:4], refs[4], refs[5], refs[6]
    rows = coef.shape[0]
    slots, tall = packed.shape[0], packed.shape[1]
    blocks = owner.shape[0]
    per_wide = slots // wide
    for k in range(4):
        for h in range(halo_blocks.shape[0]):
            at = pl.multiple_of(halo_blocks[h, k] * LANES, LANES)
            halos[k][h] = coef[:, pl.ds(at, LANES)]

    def clear(w, _):
        filled[w] = 0
        return 0

    lax.fori_loop(0, wide, clear, 0)
    if slots > blocks:
        for t in range(slots):
            packed[t, rows:tall, :] = jnp.full((tall - rows, LANES), -1, bf16)
    for b in range(blocks):
        target = owner[b]
        w = target // narrow
        t = w * per_wide + filled[w]
        filled[w] = filled[w] + 1
        slot[b] = t
        packed[t, 0:rows, :] = coef[:, b * LANES : (b + 1) * LANES]
        packed[t, rows:tall, :] = jnp.full((tall - rows, LANES), (target % narrow).astype(f32)).astype(
            bf16
        )


def pack(coef, halo_blocks, owner, wide, narrow):
    rows, count = coef.shape
    blocks = owner.shape[0]
    slots = wide * max(1, blocks // wide)
    halo = jax.ShapeDtypeStruct((halo_blocks.shape[0], rows, LANES), bf16)
    return pl.pallas_call(
        lambda *refs: pack_kernel(wide, narrow, *refs),
        out_shape=[halo] * 4
        + [
            jax.ShapeDtypeStruct((slots, padded_rows(rows), LANES), bf16),
            jax.ShapeDtypeStruct((blocks,), jnp.int32),
        ],
        in_specs=[VMEM, SMEM, SMEM],
        out_specs=[VMEM] * 5 + [SMEM],
        scratch_shapes=[pltpu.SMEM((wide,), jnp.int32)],
        cost_estimate=pl.CostEstimate(flops=0, bytes_accessed=4 * rows * count, transcendentals=0),
        compiler_params=grant(2 * rows * count, 3 * (slots + 16) * padded_rows(rows) * LANES),
        name="pack",
    )(coef, halo_blocks, owner)


def metric_kernel(nb, slot, count, coef, h0, h1, h2, h3, w, out, y0, y1, y2, y3, acc0, acc1, wp, idx, sem):
    tables = (y0, y1, y2, y3)
    accs = (acc0, acc1)
    rows = w.shape[1]
    third = rows // 3
    elems = coef.shape[1]
    blocks = elems // LANES
    contract = (((1,), (1,)), ((), ()))

    def fetch(b, place):
        at = pl.multiple_of(b * LANES, LANES)
        return pltpu.make_async_copy(nb.at[:, pl.ds(at, LANES)], idx.at[place], sem.at[place])

    for p in range(AHEAD):
        fetch(p, p).start()
    lane = lax.broadcasted_iota(jnp.int32, (LANES, rows), 0)
    row = lax.broadcasted_iota(jnp.int32, (LANES, rows), 1)
    place = ((row == 3 * (lane % 32) + lane // 32) & (lane % 32 < third)).astype(bf16)
    for f in range(FACES + 1):
        wp[f] = jnp.dot(place, w[f], preferred_element_type=f32).astype(bf16)
    step = 512

    def project(i, _):
        at = pl.multiple_of(i * step, step)
        cols = coef[:, pl.ds(at, step)].T
        for f in range(FACES):
            tables[f][pl.ds(at, step), :] = lax.dot_general(
                cols, wp[f + 1], contract, preferred_element_type=f32
            )
        return 0

    lax.fori_loop(0, elems // step, project, 0)
    for k, halo in enumerate((h0, h1, h2, h3)):
        for h in range(halo.shape[0]):
            cols = halo[h].T
            at = elems + (k * halo.shape[0] + h) * LANES
            for f in range(FACES):
                tables[f][pl.ds(at, LANES), :] = lax.dot_general(
                    cols, wp[f + 1], contract, preferred_element_type=f32
                )

    def gather(p):
        for e in range(LANES):
            part = [tables[f][pl.ds(idx[p, f, e], 1), :] for f in range(FACES)]
            accs[p % 2][pl.ds(e, 1), :] = (part[0] + part[1]) + (part[2] + part[3])

    def metric(b, p):
        at = pl.multiple_of(b * LANES, LANES)
        d = accs[p % 2][...].T + jnp.dot(
            wp[0], coef[:, pl.ds(at, LANES)], preferred_element_type=f32
        )
        x, y, z = d[0:32], d[32:64], d[64:96]
        inverse = 1.0 / third

        def mean(p):
            return inverse * jnp.sum(p, axis=0, keepdims=True)

        xx, yy, zz = 1.0 + mean(x * x), 1.0 + mean(y * y), 1.0 + mean(z * z)
        xy, xz, yz = mean(x * y), mean(x * z), mean(y * z)
        det = xx * (yy * zz - yz * yz) - xy * (xy * zz - yz * xz) + xz * (xy * yz - yy * xz)
        work = count[b].astype(f32) * jnp.sqrt(det)
        out[slot[b]] = jnp.concatenate([xx, yy, zz, xy, xz, yz, work, work], axis=0)

    def group(i, _):
        for p in range(AHEAD):
            b = AHEAD * i + p
            fetch(b, p).wait()
            gather(p)

            @pl.when(b + AHEAD < blocks)
            def _():
                fetch(b + AHEAD, p).start()

            metric(b, p)
        return 0

    lax.fori_loop(0, blocks // AHEAD, group, 0)


def metrics(nb, slot, count, coef, halos, w, slots):
    elems = coef.shape[1]
    table = elems + sum(h.shape[0] for h in halos) * LANES
    return pl.pallas_call(
        metric_kernel,
        out_shape=jax.ShapeDtypeStruct((slots, 8, LANES), f32),
        in_specs=[HBM, SMEM, SMEM] + [VMEM] * 6,
        out_specs=VMEM,
        scratch_shapes=[pltpu.VMEM((table, LANES), f32)] * FACES
        + [
            pltpu.VMEM((LANES, LANES), f32),
            pltpu.VMEM((LANES, LANES), f32),
            pltpu.VMEM((FACES + 1, LANES, w.shape[2]), bf16),
            pltpu.SMEM((AHEAD, FACES, LANES), jnp.int32),
            pltpu.SemaphoreType.DMA((AHEAD,)),
        ],
        cost_estimate=pl.CostEstimate(
            flops=2 * table * 5 * LANES * LANES, bytes_accessed=30 * elems * LANES, transcendentals=elems
        ),
        compiler_params=grant(6 * FACES * table * LANES, 2 * 104 * elems),
        name="metric",
    )(nb, slot, count, coef, *halos, w)


def relay_kernel(narrow, arrived, *refs):
    sends, order, words, tags, filled, sem = refs[:narrow], *refs[narrow:]
    slots, tall = arrived.shape[0], arrived.shape[1]
    per, rows = sends[0].shape[0], sends[0].shape[1]
    for t in range(slots):
        words[t : t + 1, :] = arrived[t, tall - 8 : tall, :].astype(f32)[7:8].astype(jnp.int32)
    copy = pltpu.make_async_copy(words, tags, sem)
    copy.start()
    copy.wait()
    for c in range(narrow + 1):
        filled[c] = c * per
    for t in range(slots):
        tag = tags[t, 0]
        c = jnp.where(tag < 0, narrow, tag)
        at = filled[c]
        order[at] = t
        filled[c] = at + 1
    mine = lax.axis_index("narrow")
    for k in range(narrow):
        for j in range(per):
            sends[k][j] = arrived[order[(mine ^ k) * per + j], 0:rows, :]


def relay(arrived, rows, narrow, blocks):
    slots = arrived.shape[0]
    per = blocks // narrow
    *sends, order = pl.pallas_call(
        lambda *refs: relay_kernel(narrow, *refs),
        out_shape=[jax.ShapeDtypeStruct((per, rows, LANES), bf16)] * narrow
        + [jax.ShapeDtypeStruct((blocks + slots,), jnp.int32)],
        in_specs=[VMEM],
        out_specs=[VMEM] * narrow + [SMEM],
        scratch_shapes=[
            pltpu.VMEM((slots, LANES), jnp.int32),
            pltpu.SMEM((slots, LANES), jnp.int32),
            pltpu.SMEM((narrow + 1,), jnp.int32),
            pltpu.SemaphoreType.DMA(()),
        ],
        cost_estimate=pl.CostEstimate(
            flops=0, bytes_accessed=4 * blocks * rows * LANES, transcendentals=0
        ),
        compiler_params=grant(3 * (slots + blocks) * padded_rows(rows) * LANES),
        name="relay",
    )(arrived)
    return sends, order


def relay_stats_kernel(narrow, arrived, order, *sends):
    per = sends[0].shape[0]
    mine = lax.axis_index("narrow")
    for k in range(narrow):
        for j in range(per):
            sends[k][j] = arrived[order[(mine ^ k) * per + j]]


def relay_stats(arrived, order, narrow, blocks):
    per = blocks // narrow
    return pl.pallas_call(
        lambda *refs: relay_stats_kernel(narrow, *refs),
        out_shape=[jax.ShapeDtypeStruct((per, 8, LANES), f32)] * narrow,
        in_specs=[VMEM, SMEM],
        out_specs=[VMEM] * narrow,
        cost_estimate=pl.CostEstimate(flops=0, bytes_accessed=64 * blocks * LANES, transcendentals=0),
        compiler_params=grant(2 * 32 * blocks * LANES),
        name="relay_stats",
    )(arrived, order)


def place_kernel(*refs):
    parts, out = refs[:-1], refs[-1]
    per = parts[0].shape[0]
    mine = lax.axis_index("narrow")
    for k, part in enumerate(parts):
        for j in range(per):
            at = pl.multiple_of(((mine ^ k) * per + j) * LANES, LANES)
            out[:, pl.ds(at, LANES)] = part[j]


def place(parts):
    per, rows, _ = parts[0].shape
    return pl.pallas_call(
        place_kernel,
        out_shape=jax.ShapeDtypeStruct((rows, len(parts) * per * LANES), bf16),
        in_specs=[VMEM] * len(parts),
        out_specs=VMEM,
        compiler_params=grant(6 * len(parts) * per * padded_rows(rows) * LANES),
        name="place",
    )(*parts)


def place_stats_kernel(*refs):
    parts, metric, work = refs[:-2], refs[-2], refs[-1]
    per = parts[0].shape[0]
    mine = lax.axis_index("narrow")
    for k, part in enumerate(parts):
        for j in range(per):
            t = (mine ^ k) * per + j
            at = pl.multiple_of(t * LANES, LANES)
            metric[:, pl.ds(at, LANES)] = part[j, 0:6, :]
            work[pl.ds(t, 1), :] = part[j, 6:7, :]


def place_stats(parts):
    per = parts[0].shape[0]
    blocks = len(parts) * per
    return pl.pallas_call(
        place_stats_kernel,
        out_shape=[
            jax.ShapeDtypeStruct((6, blocks * LANES), f32),
            jax.ShapeDtypeStruct((blocks, LANES), f32),
        ],
        in_specs=[VMEM] * len(parts),
        out_specs=[VMEM] * 2,
        compiler_params=grant(3 * 32 * blocks * LANES),
        name="place_stats",
    )(*parts)


def per_device(coefficients, neighbours, halo_blocks, recon_weight, owner_device, work_count):
    wide = lax.axis_size("wide")
    narrow = lax.axis_size("narrow")
    rows, _ = coefficients.shape
    blocks = owner_device.shape[0]
    to0, to1, to2, to3, packed, slot = pack(
        coefficients, halo_blocks[0].T, owner_device, wide, narrow
    )
    halos = [
        passed_along(to1, "wide", 1),
        passed_along(to0, "wide", -1),
        passed_along(to3, "narrow", 1),
        passed_along(to2, "narrow", -1),
    ]
    arrived = lax.all_to_all(packed, "wide", 0, 0, tiled=True)
    stats = metrics(
        neighbours, slot, work_count, coefficients, halos, recon_weight, packed.shape[0]
    )
    stats_arrived = lax.all_to_all(stats, "wide", 0, 0, tiled=True)
    sends, order = relay(arrived, rows, narrow, blocks)
    parts = [sends[0]] + [swapped(sends[k], "narrow", k) for k in range(1, narrow)]
    stats_sends = relay_stats(stats_arrived, order, narrow, blocks)
    stats_parts = [stats_sends[0]] + [
        swapped(stats_sends[k], "narrow", k) for k in range(1, narrow)
    ]
    modal = place(parts)
    metric, work = place_stats(stats_parts)
    return modal, metric, work.reshape(-1)


def solution(mesh):
    return jax.shard_map(
        per_device,
        mesh=mesh,
        in_specs=(
            P(None, ("wide", "narrow")),
            P(None, ("wide", "narrow")),
            P(("wide", "narrow"), None, None),
            P(),
            P(("wide", "narrow")),
            P(("wide", "narrow")),
        ),
        out_specs=(P(None, ("wide", "narrow")), P(None, ("wide", "narrow")), P(("wide", "narrow"))),
        check_vma=False,
    )
```

```python
import jax
import jax.numpy as jnp
from jax import lax
from jax.experimental import pallas as pl
from jax.experimental.pallas import tpu as pltpu
from jax.sharding import PartitionSpec as P

f32 = jnp.float32
bf16 = jnp.bfloat16
LANES = 128
FACES = 4
AHEAD = 4
THIRD = 32

SMEM = pl.BlockSpec(memory_space=pltpu.SMEM)
VMEM = pl.BlockSpec(memory_space=pltpu.VMEM)
HBM = pl.BlockSpec(memory_space=pltpu.HBM)


def grant(*shapes):
    return pltpu.CompilerParams(vmem_limit_bytes=sum(shapes) + (1 << 20))


def far_pairs(value, axis):
    count = lax.axis_size(axis)
    return lax.ppermute(
        value, axis, [(at, (at + (1 if at % 2 else -1)) % count) for at in range(count)]
    )


def swapped(value, axis, flip):
    count = lax.axis_size(axis)
    return lax.ppermute(value, axis, [(source, source ^ flip) for source in range(count)])


def padded_rows(rows):
    return (rows // 8 + 1) * 8


def sides():
    odd_wide = lax.axis_index("wide") % 2
    odd_narrow = lax.axis_index("narrow") % 2
    return odd_wide, 1 - odd_wide, 2 + odd_narrow, 3 - odd_narrow


def halo_kernel(coef, halo_blocks, *refs):
    outs, sems = refs[:4], refs[4]
    copies = []
    for k, side in enumerate(sides()):
        for h in range(outs[k].shape[0]):
            at = pl.multiple_of(halo_blocks[h, side] * LANES, LANES)
            copies.append(
                pltpu.make_async_copy(coef.at[:, pl.ds(at, LANES)], outs[k].at[h], sems.at[k, h])
            )
    for copy in copies:
        copy.start()
    for copy in copies:
        copy.wait()


def halo_pack(coef, halo_blocks):
    rows = coef.shape[0]
    count = halo_blocks.shape[0]
    return pl.pallas_call(
        halo_kernel,
        out_shape=[jax.ShapeDtypeStruct((count, rows, LANES), bf16)] * 4,
        in_specs=[HBM, SMEM],
        out_specs=[VMEM] * 4,
        scratch_shapes=[pltpu.SemaphoreType.DMA((4, count))],
        cost_estimate=pl.CostEstimate(
            flops=0, bytes_accessed=16 * count * rows * LANES, transcendentals=0
        ),
        compiler_params=grant(16 * count * padded_rows(rows) * LANES),
        name="halo_pack",
    )(coef, halo_blocks)


def stats_place(t, w, per_wide, slots):
    away = (w ^ lax.axis_index("wide")) % 2
    return away * (slots // 2) + (w // 2) * per_wide + t % per_wide


def pack_kernel(wide, narrow, coef, owner, count, packed, route, filled):
    rows = coef.shape[0]
    slots, tall = packed.shape[0], packed.shape[1]
    blocks = owner.shape[0]
    per_wide = slots // wide

    def clear(w, _):
        filled[w] = 0
        return 0

    lax.fori_loop(0, wide, clear, 0)
    if slots > blocks:
        for t in range(slots):
            packed[t, rows:tall, :] = jnp.full((tall - rows, LANES), -1, bf16)
    for b in range(blocks):
        target = owner[b]
        w = target // narrow
        t = w * per_wide + filled[w]
        filled[w] = filled[w] + 1
        route[0, b] = stats_place(t, w, per_wide, slots) if slots == blocks else t
        route[1, b] = count[b]
        packed[t, 0:rows, :] = coef[:, b * LANES : (b + 1) * LANES]
        packed[t, rows:tall, :] = jnp.full((tall - rows, LANES), (target % narrow).astype(f32)).astype(
            bf16
        )


def pack(coef, owner, count, wide, narrow):
    rows, elems = coef.shape
    blocks = owner.shape[0]
    slots = wide * max(1, blocks // wide)
    return pl.pallas_call(
        lambda *refs: pack_kernel(wide, narrow, *refs),
        out_shape=[
            jax.ShapeDtypeStruct((slots, padded_rows(rows), LANES), bf16),
            jax.ShapeDtypeStruct((2, blocks), jnp.int32),
        ],
        in_specs=[VMEM, SMEM, SMEM],
        out_specs=[VMEM, SMEM],
        scratch_shapes=[pltpu.SMEM((wide,), jnp.int32)],
        cost_estimate=pl.CostEstimate(flops=0, bytes_accessed=4 * rows * elems, transcendentals=0),
        compiler_params=grant(2 * rows * elems, 3 * slots * padded_rows(rows) * LANES),
        name="pack",
    )(coef, owner, count)


def metric_kernel(nb, routes, coef, h0, h1, h2, h3, w, *refs):
    *outs, table, accs, wp, idx, sem, stats, route, arrived = refs
    rows, depth = w.shape[1], w.shape[2]
    third = rows // 3
    elems = coef.shape[1]
    groups = elems // (AHEAD * LANES)

    def fetch(g, s):
        at = pl.multiple_of(g * (AHEAD * LANES), LANES)
        return pltpu.make_async_copy(nb.at[:, pl.ds(at, AHEAD * LANES)], idx.at[s], sem.at[s])

    fetch(0, 0).start()
    fetch(1, 1).start()
    routing = pltpu.make_async_copy(routes, route, arrived)
    routing.start()
    line = lax.broadcasted_iota(jnp.int32, (3 * THIRD, rows), 0)
    row = lax.broadcasted_iota(jnp.int32, (3 * THIRD, rows), 1)
    order = ((row == 3 * (line % THIRD) + line // THIRD) & (line % THIRD < third)).astype(bf16)
    spare = jnp.zeros((3 * THIRD, LANES - depth), bf16)
    for f in range(FACES + 1):
        ordered = jnp.dot(order, w[f], preferred_element_type=f32).astype(bf16)
        wp[:, f * LANES : (f + 1) * LANES] = jnp.concatenate([ordered, spare], axis=1)

    def by_element(cols):
        turned = cols.astype(f32).T
        return jnp.concatenate([turned, jnp.zeros((turned.shape[0], LANES - depth), f32)], axis=1)

    step = 512

    def fill(i, _):
        at = pl.multiple_of(i * step, step)
        table[pl.ds(at, step), :] = by_element(coef[:, pl.ds(at, step)])
        return 0

    lax.fori_loop(0, elems // step, fill, 0)
    for side, halo in zip(sides(), (h0, h1, h2, h3)):
        for h in range(halo.shape[0]):
            at = pl.multiple_of(elems + (side * halo.shape[0] + h) * LANES, LANES)
            table[pl.ds(at, LANES), :] = by_element(halo[h])

    def gather(s, p):
        for e in range(LANES):
            for f in range(FACES):
                accs[s * AHEAD + p, pl.ds(e, 1), f * LANES : (f + 1) * LANES] = table[
                    pl.ds(idx[s, f, p * LANES + e], 1), :
                ]

    def metric(b, s, p):
        at = pl.multiple_of(b * LANES, LANES)
        d = jnp.dot(
            wp[:, 0:depth], coef[:, pl.ds(at, LANES)], preferred_element_type=f32
        ) + lax.dot_general(
            wp[:, LANES:],
            accs[s * AHEAD + p].astype(bf16),
            (((1,), (1,)), ((), ())),
            preferred_element_type=f32,
        )
        x, y, z = d[0:THIRD], d[THIRD : 2 * THIRD], d[2 * THIRD :]
        inverse = 1.0 / third

        def mean(p):
            return inverse * jnp.sum(p, axis=0, keepdims=True)

        xx, yy, zz = 1.0 + mean(x * x), 1.0 + mean(y * y), 1.0 + mean(z * z)
        xy, xz, yz = mean(x * y), mean(x * z), mean(y * z)
        det = xx * (yy * zz - yz * yz) - xy * (xy * zz - yz * xz) + xz * (xy * yz - yy * xz)
        work = route[1, b].astype(f32) * jnp.sqrt(det)
        stats[route[0, b]] = jnp.concatenate([xx, yy, zz, xy, xz, yz, work, work], axis=0)

    routing.wait()

    def two_groups(i, _):
        for s in range(2):
            g = 2 * i + s
            earlier = jnp.maximum(g - 1, 0) if s == 0 else g - 1
            fetch(g, s).wait()
            for p in range(AHEAD):
                metric(earlier * AHEAD + p, 1 - s, p)
                gather(s, p)
            fetch(jnp.minimum(g + 2, groups - 1), s).start()
        return 0

    lax.fori_loop(0, groups // 2, two_groups, 0)
    for p in range(AHEAD):
        metric((groups - 1) * AHEAD + p, 1, p)
    for s in range(2):
        fetch(groups - 1, s).wait()
    size = outs[0].shape[0]
    for k, out in enumerate(outs):
        out[...] = stats[k * size : (k + 1) * size]


def metrics(nb, route, coef, halos, w, slots):
    elems = coef.shape[1]
    table = elems + sum(h.shape[0] for h in halos) * LANES
    parts = 2 if slots == elems // LANES else 1
    return pl.pallas_call(
        metric_kernel,
        out_shape=[jax.ShapeDtypeStruct((slots // parts, 8, LANES), f32)] * parts,
        in_specs=[HBM, HBM] + [VMEM] * 6,
        out_specs=[VMEM] * parts,
        scratch_shapes=[
            pltpu.VMEM((table, LANES), f32),
            pltpu.VMEM((2 * AHEAD, LANES, FACES * LANES), f32),
            pltpu.VMEM((3 * THIRD, (FACES + 1) * LANES), bf16),
            pltpu.SMEM((2, FACES, AHEAD * LANES), jnp.int32),
            pltpu.SemaphoreType.DMA((2,)),
            pltpu.VMEM((slots, 8, LANES), f32),
            pltpu.SMEM(route.shape, jnp.int32),
            pltpu.SemaphoreType.DMA(()),
        ],
        cost_estimate=pl.CostEstimate(
            flops=2 * elems * 5 * LANES * LANES, bytes_accessed=20 * elems * LANES, transcendentals=elems
        ),
        compiler_params=grant(4 * table * LANES, 3 * 104 * elems, 96 * slots * LANES, 5 << 20),
        name="metric",
    )(nb, route, coef, *halos, w)


def relay_kernel(narrow, arrived, *refs):
    sends, order, words, tags, filled, sem = refs[:narrow], *refs[narrow:]
    slots, tall = arrived.shape[0], arrived.shape[1]
    per, rows = sends[0].shape[0], sends[0].shape[1]
    for t in range(slots):
        words[t : t + 1, :] = arrived[t, tall - 8 : tall, :].astype(f32)[7:8].astype(jnp.int32)
    copy = pltpu.make_async_copy(words, tags, sem)
    copy.start()
    copy.wait()
    for c in range(narrow + 1):
        filled[c] = c * per
    for t in range(slots):
        tag = tags[t, 0]
        c = jnp.where(tag < 0, narrow, tag)
        at = filled[c]
        order[at] = t
        filled[c] = at + 1
    mine = lax.axis_index("narrow")
    for k in range(narrow):
        for j in range(per):
            sends[k][j] = arrived[order[(mine ^ k) * per + j], 0:rows, :]


def relay(arrived, rows, narrow, blocks):
    slots = arrived.shape[0]
    per = blocks // narrow
    *sends, order = pl.pallas_call(
        lambda *refs: relay_kernel(narrow, *refs),
        out_shape=[jax.ShapeDtypeStruct((per, rows, LANES), bf16)] * narrow
        + [jax.ShapeDtypeStruct((blocks + slots,), jnp.int32)],
        in_specs=[VMEM],
        out_specs=[VMEM] * narrow + [SMEM],
        scratch_shapes=[
            pltpu.VMEM((slots, LANES), jnp.int32),
            pltpu.SMEM((slots, LANES), jnp.int32),
            pltpu.SMEM((narrow + 1,), jnp.int32),
            pltpu.SemaphoreType.DMA(()),
        ],
        cost_estimate=pl.CostEstimate(
            flops=0, bytes_accessed=4 * blocks * rows * LANES, transcendentals=0
        ),
        compiler_params=grant(3 * (slots + blocks) * padded_rows(rows) * LANES),
        name="relay",
    )(arrived)
    return sends, order


def merge_kernel(kept, got, *sends):
    per = sends[0].shape[0] // 2
    mine = lax.axis_index("wide") // 2
    for j, send in enumerate(sends):
        at = (mine ^ j) * per
        for i in range(per):
            send[i] = kept[at + i]
            send[per + i] = got[at + i]


def merge(kept, got, wide):
    half = kept.shape[0]
    groups = wide // 2
    return pl.pallas_call(
        merge_kernel,
        out_shape=[jax.ShapeDtypeStruct((2 * half // groups, 8, LANES), f32)] * groups,
        in_specs=[VMEM] * 2,
        out_specs=[VMEM] * groups,
        cost_estimate=pl.CostEstimate(flops=0, bytes_accessed=128 * half * LANES, transcendentals=0),
        compiler_params=grant(4 * 64 * half * LANES),
        name="merge",
    )(kept, got)


def relay_stats_kernel(narrow, per_wide, *refs):
    parts, order, sends, held = refs[: -narrow - 2], refs[-narrow - 2], refs[-narrow - 1 : -1], refs[-1]
    per = sends[0].shape[0]
    mine = lax.axis_index("narrow")
    wide = lax.axis_index("wide")
    size = parts[0].shape[0]
    for j, part in enumerate(parts):
        held[j * size : (j + 1) * size] = part[...]
    for k in range(narrow):
        for j in range(per):
            t = order[(mine ^ k) * per + j]
            if len(parts) > 1:
                t = ((t // per_wide) ^ wide) * per_wide + t % per_wide
            sends[k][j] = held[t]


def relay_stats(parts, order, narrow, per_wide, blocks):
    per = blocks // narrow
    slots = len(parts) * parts[0].shape[0]
    return pl.pallas_call(
        lambda *refs: relay_stats_kernel(narrow, per_wide, *refs),
        out_shape=[jax.ShapeDtypeStruct((per, 8, LANES), f32)] * narrow,
        in_specs=[VMEM] * len(parts) + [SMEM],
        out_specs=[VMEM] * narrow,
        scratch_shapes=[pltpu.VMEM((slots, 8, LANES), f32)],
        cost_estimate=pl.CostEstimate(flops=0, bytes_accessed=64 * slots * LANES, transcendentals=0),
        compiler_params=grant(4 * 32 * (slots + blocks) * LANES),
        name="relay_stats",
    )(*parts, order)


def place_kernel(*refs):
    parts, out = refs[:-1], refs[-1]
    per = parts[0].shape[0]
    mine = lax.axis_index("narrow")
    for k, part in enumerate(parts):
        for j in range(per):
            at = pl.multiple_of(((mine ^ k) * per + j) * LANES, LANES)
            out[:, pl.ds(at, LANES)] = part[j]


def place(parts):
    per, rows, _ = parts[0].shape
    return pl.pallas_call(
        place_kernel,
        out_shape=jax.ShapeDtypeStruct((rows, len(parts) * per * LANES), bf16),
        in_specs=[VMEM] * len(parts),
        out_specs=VMEM,
        compiler_params=grant(6 * len(parts) * per * padded_rows(rows) * LANES),
        name="place",
    )(*parts)


def place_stats_kernel(*refs):
    parts, metric, work = refs[:-2], refs[-2], refs[-1]
    per = parts[0].shape[0]
    mine = lax.axis_index("narrow")
    for k, part in enumerate(parts):
        for j in range(per):
            t = (mine ^ k) * per + j
            at = pl.multiple_of(t * LANES, LANES)
            metric[:, pl.ds(at, LANES)] = part[j, 0:6, :]
            work[pl.ds(t, 1), :] = part[j, 6:7, :]


def place_stats(parts):
    per = parts[0].shape[0]
    blocks = len(parts) * per
    return pl.pallas_call(
        place_stats_kernel,
        out_shape=[
            jax.ShapeDtypeStruct((6, blocks * LANES), f32),
            jax.ShapeDtypeStruct((blocks, LANES), f32),
        ],
        in_specs=[VMEM] * len(parts),
        out_specs=[VMEM] * 2,
        compiler_params=grant(3 * 32 * blocks * LANES),
        name="place_stats",
    )(*parts)


def per_device(coefficients, neighbours, halo_blocks, recon_weight, owner_device, work_count):
    wide = lax.axis_size("wide")
    narrow = lax.axis_size("narrow")
    rows, _ = coefficients.shape
    blocks = owner_device.shape[0]
    sent = halo_pack(coefficients, halo_blocks[0].T)
    halos = [
        far_pairs(sent[0], "wide"),
        swapped(sent[1], "wide", 1),
        far_pairs(sent[2], "narrow"),
        swapped(sent[3], "narrow", 1),
    ]
    packed, route = pack(coefficients, owner_device, work_count, wide, narrow)
    slots = packed.shape[0]
    arrived = lax.all_to_all(packed, "wide", 0, 0, tiled=True)
    stats = metrics(neighbours, route, coefficients, halos, recon_weight, slots)
    if len(stats) == 1:
        stats_arrived = [lax.all_to_all(stats[0], "wide", 0, 0, tiled=True)]
    else:
        got = swapped(stats[1], "wide", 1)
        stats_arrived = list(merge(stats[0], got, wide))
        for j in range(1, wide // 2):
            stats_arrived[j] = swapped(stats_arrived[j], "wide", 2 * j)
    sends, order = relay(arrived, rows, narrow, blocks)
    parts = [sends[0]] + [swapped(sends[k], "narrow", k) for k in range(1, narrow)]
    stats_sends = relay_stats(stats_arrived, order, narrow, slots // wide, blocks)
    stats_parts = [stats_sends[0]] + [
        swapped(stats_sends[k], "narrow", k) for k in range(1, narrow)
    ]
    modal = place(parts)
    metric, work = place_stats(stats_parts)
    return modal, metric, work.reshape(-1)


def solution(mesh):
    return jax.shard_map(
        per_device,
        mesh=mesh,
        in_specs=(
            P(None, ("wide", "narrow")),
            P(None, ("wide", "narrow")),
            P(("wide", "narrow"), None, None),
            P(),
            P(("wide", "narrow")),
            P(("wide", "narrow")),
        ),
        out_specs=(P(None, ("wide", "narrow")), P(None, ("wide", "narrow")), P(("wide", "narrow"))),
        check_vma=False,
    )
```

```python
import jax
import jax.numpy as jnp
from jax import lax
from jax.experimental import pallas as pl
from jax.experimental.pallas import tpu as pltpu
from jax.sharding import PartitionSpec as P

f32 = jnp.float32
bf16 = jnp.bfloat16
LANES = 128
FACES = 4
AHEAD = 4
THIRD = 32

SMEM = pl.BlockSpec(memory_space=pltpu.SMEM)
VMEM = pl.BlockSpec(memory_space=pltpu.VMEM)
HBM = pl.BlockSpec(memory_space=pltpu.HBM)


def grant(*shapes):
    return pltpu.CompilerParams(vmem_limit_bytes=sum(shapes) + (1 << 20))


def far_pairs(value, axis):
    count = lax.axis_size(axis)
    return lax.ppermute(
        value, axis, [(at, (at + (1 if at % 2 else -1)) % count) for at in range(count)]
    )


def swapped(value, axis, flip):
    count = lax.axis_size(axis)
    return lax.ppermute(value, axis, [(source, source ^ flip) for source in range(count)])


def padded_rows(rows):
    return (rows // 8 + 1) * 8


def sides():
    odd_wide = lax.axis_index("wide") % 2
    odd_narrow = lax.axis_index("narrow") % 2
    return odd_wide, 1 - odd_wide, 2 + odd_narrow, 3 - odd_narrow


def halo_kernel(coef, listed, *refs):
    *outs, held, halo_blocks, sems = refs
    copies = [
        pltpu.make_async_copy(listed, halo_blocks, sems.at[0]),
        pltpu.make_async_copy(coef, held, sems.at[1]),
    ]
    for copy in copies:
        copy.start()
    for copy in copies:
        copy.wait()
    for k, side in enumerate(sides()):
        for h in range(outs[k].shape[0]):
            at = pl.multiple_of(halo_blocks[h, side] * LANES, LANES)
            outs[k][h] = held[:, pl.ds(at, LANES)]


def halo_pack(coef, halo_blocks):
    rows, elems = coef.shape
    count = halo_blocks.shape[0]
    return pl.pallas_call(
        halo_kernel,
        out_shape=[jax.ShapeDtypeStruct((count, rows, LANES), bf16)] * 4
        + [jax.ShapeDtypeStruct((rows, elems), bf16)],
        in_specs=[HBM, HBM],
        out_specs=[VMEM] * 5,
        scratch_shapes=[
            pltpu.SMEM(halo_blocks.shape, jnp.int32),
            pltpu.SemaphoreType.DMA((2,)),
        ],
        cost_estimate=pl.CostEstimate(
            flops=0, bytes_accessed=4 * rows * elems, transcendentals=0
        ),
        compiler_params=grant(4 * padded_rows(rows) * (elems + 4 * count * LANES)),
        name="halo_pack",
    )(
        pltpu.with_memory_space_constraint(coef, pltpu.HBM),
        pltpu.with_memory_space_constraint(halo_blocks, pltpu.HBM),
    )


def stats_place(t, w, per_wide, slots):
    away = (w ^ lax.axis_index("wide")) % 2
    return away * (slots // 2) + (w // 2) * per_wide + t % per_wide


def pack_kernel(wide, narrow, coef, owner, count, packed, route, filled):
    rows = coef.shape[0]
    slots, tall = packed.shape[0], packed.shape[1]
    blocks = owner.shape[0]
    per_wide = slots // wide

    def clear(w, _):
        filled[w] = 0
        return 0

    lax.fori_loop(0, wide, clear, 0)
    if slots > blocks:
        for t in range(slots):
            packed[t, rows:tall, :] = jnp.full((tall - rows, LANES), -1, bf16)
    for b in range(blocks):
        target = owner[b]
        w = target // narrow
        t = w * per_wide + filled[w]
        filled[w] = filled[w] + 1
        route[0, b] = stats_place(t, w, per_wide, slots) if slots == blocks else t
        route[1, b] = count[b]
        packed[t, 0:rows, :] = coef[:, b * LANES : (b + 1) * LANES]
        packed[t, rows:tall, :] = jnp.full((tall - rows, LANES), (target % narrow).astype(f32)).astype(
            bf16
        )


def pack(coef, owner, count, wide, narrow):
    rows, elems = coef.shape
    blocks = owner.shape[0]
    slots = wide * max(1, blocks // wide)
    return pl.pallas_call(
        lambda *refs: pack_kernel(wide, narrow, *refs),
        out_shape=[
            jax.ShapeDtypeStruct((slots, padded_rows(rows), LANES), bf16),
            jax.ShapeDtypeStruct((2, blocks), jnp.int32),
        ],
        in_specs=[VMEM, SMEM, SMEM],
        out_specs=[VMEM, SMEM],
        scratch_shapes=[pltpu.SMEM((wide,), jnp.int32)],
        cost_estimate=pl.CostEstimate(flops=0, bytes_accessed=4 * rows * elems, transcendentals=0),
        compiler_params=grant(2 * rows * elems, 3 * slots * padded_rows(rows) * LANES),
        name="pack",
    )(coef, owner, count)


def metric_kernel(nb, routes, coef, h0, h1, h2, h3, w, *refs):
    *outs, table, accs, wp, idx, sem, stats, route, arrived = refs
    rows, depth = w.shape[1], w.shape[2]
    third = rows // 3
    elems = coef.shape[1]
    groups = elems // (AHEAD * LANES)

    def fetch(g, s):
        at = pl.multiple_of(g * (AHEAD * LANES), LANES)
        return pltpu.make_async_copy(nb.at[:, pl.ds(at, AHEAD * LANES)], idx.at[s], sem.at[s])

    fetch(0, 0).start()
    fetch(1, 1).start()
    routing = pltpu.make_async_copy(routes, route, arrived)
    routing.start()
    line = lax.broadcasted_iota(jnp.int32, (3 * THIRD, rows), 0)
    row = lax.broadcasted_iota(jnp.int32, (3 * THIRD, rows), 1)
    order = ((row == 3 * (line % THIRD) + line // THIRD) & (line % THIRD < third)).astype(bf16)
    spare = jnp.zeros((3 * THIRD, LANES - depth), bf16)
    for f in range(FACES + 1):
        ordered = jnp.dot(order, w[f], preferred_element_type=f32).astype(bf16)
        wp[:, f * LANES : (f + 1) * LANES] = jnp.concatenate([ordered, spare], axis=1)

    def by_element(cols):
        turned = cols.astype(f32).T
        return jnp.concatenate([turned, jnp.zeros((turned.shape[0], LANES - depth), f32)], axis=1)

    step = 512

    def fill(i, _):
        at = pl.multiple_of(i * step, step)
        table[pl.ds(at, step), :] = by_element(coef[:, pl.ds(at, step)])
        return 0

    lax.fori_loop(0, elems // step, fill, 0)
    for side, halo in zip(sides(), (h0, h1, h2, h3)):
        for h in range(halo.shape[0]):
            at = pl.multiple_of(elems + (side * halo.shape[0] + h) * LANES, LANES)
            table[pl.ds(at, LANES), :] = by_element(halo[h])

    def gather(s, p):
        for e in range(LANES):
            for f in range(FACES):
                accs[s * AHEAD + p, pl.ds(e, 1), f * LANES : (f + 1) * LANES] = table[
                    pl.ds(idx[s, f, p * LANES + e], 1), :
                ]

    def metric(b, s, p):
        at = pl.multiple_of(b * LANES, LANES)
        d = jnp.dot(
            wp[:, 0:depth], coef[:, pl.ds(at, LANES)], preferred_element_type=f32
        ) + lax.dot_general(
            wp[:, LANES:],
            accs[s * AHEAD + p].astype(bf16),
            (((1,), (1,)), ((), ())),
            preferred_element_type=f32,
        )
        x, y, z = d[0:THIRD], d[THIRD : 2 * THIRD], d[2 * THIRD :]
        inverse = 1.0 / third

        def mean(p):
            return inverse * jnp.sum(p, axis=0, keepdims=True)

        xx, yy, zz = 1.0 + mean(x * x), 1.0 + mean(y * y), 1.0 + mean(z * z)
        xy, xz, yz = mean(x * y), mean(x * z), mean(y * z)
        det = xx * (yy * zz - yz * yz) - xy * (xy * zz - yz * xz) + xz * (xy * yz - yy * xz)
        work = route[1, b].astype(f32) * jnp.sqrt(det)
        stats[route[0, b]] = jnp.concatenate([xx, yy, zz, xy, xz, yz, work, work], axis=0)

    routing.wait()

    def two_groups(i, _):
        for s in range(2):
            g = 2 * i + s
            earlier = jnp.maximum(g - 1, 0) if s == 0 else g - 1
            fetch(g, s).wait()
            for p in range(AHEAD):
                metric(earlier * AHEAD + p, 1 - s, p)
                gather(s, p)
            fetch(jnp.minimum(g + 2, groups - 1), s).start()
        return 0

    lax.fori_loop(0, groups // 2, two_groups, 0)
    for p in range(AHEAD):
        metric((groups - 1) * AHEAD + p, 1, p)
    for s in range(2):
        fetch(groups - 1, s).wait()
    size = outs[0].shape[0]
    for k, out in enumerate(outs):
        out[...] = stats[k * size : (k + 1) * size]


def metrics(nb, route, coef, halos, w, slots):
    elems = coef.shape[1]
    table = elems + sum(h.shape[0] for h in halos) * LANES
    parts = 2 if slots == elems // LANES else 1
    return pl.pallas_call(
        metric_kernel,
        out_shape=[jax.ShapeDtypeStruct((slots // parts, 8, LANES), f32)] * parts,
        in_specs=[HBM, HBM] + [VMEM] * 6,
        out_specs=[VMEM] * parts,
        scratch_shapes=[
            pltpu.VMEM((table, LANES), f32),
            pltpu.VMEM((2 * AHEAD, LANES, FACES * LANES), f32),
            pltpu.VMEM((3 * THIRD, (FACES + 1) * LANES), bf16),
            pltpu.SMEM((2, FACES, AHEAD * LANES), jnp.int32),
            pltpu.SemaphoreType.DMA((2,)),
            pltpu.VMEM((slots, 8, LANES), f32),
            pltpu.SMEM(route.shape, jnp.int32),
            pltpu.SemaphoreType.DMA(()),
        ],
        cost_estimate=pl.CostEstimate(
            flops=2 * elems * 5 * LANES * LANES, bytes_accessed=20 * elems * LANES, transcendentals=elems
        ),
        compiler_params=grant(4 * table * LANES, 3 * 104 * elems, 96 * slots * LANES, 5 << 20),
        name="metric",
    )(nb, route, coef, *halos, w)


def relay_kernel(narrow, arrived, *refs):
    sends, order, words, tags, filled, sem = refs[:narrow], *refs[narrow:]
    slots, tall = arrived.shape[0], arrived.shape[1]
    per, rows = sends[0].shape[0], sends[0].shape[1]
    for t in range(slots):
        words[t : t + 1, :] = arrived[t, tall - 8 : tall, :].astype(f32)[7:8].astype(jnp.int32)
    copy = pltpu.make_async_copy(words, tags, sem)
    copy.start()
    copy.wait()
    for c in range(narrow + 1):
        filled[c] = c * per
    for t in range(slots):
        tag = tags[t, 0]
        c = jnp.where(tag < 0, narrow, tag)
        at = filled[c]
        order[at] = t
        filled[c] = at + 1
    mine = lax.axis_index("narrow")
    for k in range(narrow):
        for j in range(per):
            sends[k][j] = arrived[order[(mine ^ k) * per + j], 0:rows, :]


def relay(arrived, rows, narrow, blocks):
    slots = arrived.shape[0]
    per = blocks // narrow
    *sends, order = pl.pallas_call(
        lambda *refs: relay_kernel(narrow, *refs),
        out_shape=[jax.ShapeDtypeStruct((per, rows, LANES), bf16)] * narrow
        + [jax.ShapeDtypeStruct((blocks + slots,), jnp.int32)],
        in_specs=[VMEM],
        out_specs=[VMEM] * narrow + [SMEM],
        scratch_shapes=[
            pltpu.VMEM((slots, LANES), jnp.int32),
            pltpu.SMEM((slots, LANES), jnp.int32),
            pltpu.SMEM((narrow + 1,), jnp.int32),
            pltpu.SemaphoreType.DMA(()),
        ],
        cost_estimate=pl.CostEstimate(
            flops=0, bytes_accessed=4 * blocks * rows * LANES, transcendentals=0
        ),
        compiler_params=grant(3 * (slots + blocks) * padded_rows(rows) * LANES),
        name="relay",
    )(arrived)
    return sends, order


def merge_kernel(kept, got, *sends):
    per = sends[0].shape[0] // 2
    mine = lax.axis_index("wide") // 2
    for j, send in enumerate(sends):
        at = (mine ^ j) * per
        for i in range(per):
            send[i] = kept[at + i]
            send[per + i] = got[at + i]


def merge(kept, got, wide):
    half = kept.shape[0]
    groups = wide // 2
    return pl.pallas_call(
        merge_kernel,
        out_shape=[jax.ShapeDtypeStruct((2 * half // groups, 8, LANES), f32)] * groups,
        in_specs=[VMEM] * 2,
        out_specs=[VMEM] * groups,
        cost_estimate=pl.CostEstimate(flops=0, bytes_accessed=128 * half * LANES, transcendentals=0),
        compiler_params=grant(4 * 64 * half * LANES),
        name="merge",
    )(kept, got)


def relay_stats_kernel(narrow, per_wide, *refs):
    parts, order, sends, held = refs[: -narrow - 2], refs[-narrow - 2], refs[-narrow - 1 : -1], refs[-1]
    per = sends[0].shape[0]
    mine = lax.axis_index("narrow")
    wide = lax.axis_index("wide")
    size = parts[0].shape[0]
    for j, part in enumerate(parts):
        held[j * size : (j + 1) * size] = part[...]
    for k in range(narrow):
        for j in range(per):
            t = order[(mine ^ k) * per + j]
            if len(parts) > 1:
                t = ((t // per_wide) ^ wide) * per_wide + t % per_wide
            sends[k][j] = held[t]


def relay_stats(parts, order, narrow, per_wide, blocks):
    per = blocks // narrow
    slots = len(parts) * parts[0].shape[0]
    return pl.pallas_call(
        lambda *refs: relay_stats_kernel(narrow, per_wide, *refs),
        out_shape=[jax.ShapeDtypeStruct((per, 8, LANES), f32)] * narrow,
        in_specs=[VMEM] * len(parts) + [SMEM],
        out_specs=[VMEM] * narrow,
        scratch_shapes=[pltpu.VMEM((slots, 8, LANES), f32)],
        cost_estimate=pl.CostEstimate(flops=0, bytes_accessed=64 * slots * LANES, transcendentals=0),
        compiler_params=grant(4 * 32 * (slots + blocks) * LANES),
        name="relay_stats",
    )(*parts, order)


def place_kernel(*refs):
    parts, out = refs[:-1], refs[-1]
    per = parts[0].shape[0]
    mine = lax.axis_index("narrow")
    for k, part in enumerate(parts):
        for j in range(per):
            at = pl.multiple_of(((mine ^ k) * per + j) * LANES, LANES)
            out[:, pl.ds(at, LANES)] = part[j]


def place(parts):
    per, rows, _ = parts[0].shape
    return pl.pallas_call(
        place_kernel,
        out_shape=jax.ShapeDtypeStruct((rows, len(parts) * per * LANES), bf16),
        in_specs=[VMEM] * len(parts),
        out_specs=VMEM,
        compiler_params=grant(6 * len(parts) * per * padded_rows(rows) * LANES),
        name="place",
    )(*parts)


def place_stats_kernel(*refs):
    parts, metric, work = refs[:-2], refs[-2], refs[-1]
    per = parts[0].shape[0]
    mine = lax.axis_index("narrow")
    for k, part in enumerate(parts):
        for j in range(per):
            t = (mine ^ k) * per + j
            at = pl.multiple_of(t * LANES, LANES)
            metric[:, pl.ds(at, LANES)] = part[j, 0:6, :]
            work[pl.ds(t, 1), :] = part[j, 6:7, :]


def place_stats(parts):
    per = parts[0].shape[0]
    blocks = len(parts) * per
    return pl.pallas_call(
        place_stats_kernel,
        out_shape=[
            jax.ShapeDtypeStruct((6, blocks * LANES), f32),
            jax.ShapeDtypeStruct((blocks, LANES), f32),
        ],
        in_specs=[VMEM] * len(parts),
        out_specs=[VMEM] * 2,
        compiler_params=grant(3 * 32 * blocks * LANES),
        name="place_stats",
    )(*parts)


def per_device(coefficients, neighbours, halo_blocks, recon_weight, owner_device, work_count):
    wide = lax.axis_size("wide")
    narrow = lax.axis_size("narrow")
    rows, _ = coefficients.shape
    blocks = owner_device.shape[0]
    *sent, held = halo_pack(coefficients, halo_blocks[0].T)
    halos = [
        far_pairs(sent[0], "wide"),
        swapped(sent[1], "wide", 1),
        far_pairs(sent[2], "narrow"),
        swapped(sent[3], "narrow", 1),
    ]
    packed, route = pack(held, owner_device, work_count, wide, narrow)
    slots = packed.shape[0]
    arrived = lax.all_to_all(packed, "wide", 0, 0, tiled=True)
    stats = metrics(neighbours, route, held, halos, recon_weight, slots)
    if len(stats) == 1:
        stats_arrived = [lax.all_to_all(stats[0], "wide", 0, 0, tiled=True)]
    else:
        got = swapped(stats[1], "wide", 1)
        stats_arrived = list(merge(stats[0], got, wide))
        for j in range(1, wide // 2):
            stats_arrived[j] = swapped(stats_arrived[j], "wide", 2 * j)
    sends, order = relay(arrived, rows, narrow, blocks)
    parts = [sends[0]] + [swapped(sends[k], "narrow", k) for k in range(1, narrow)]
    stats_sends = relay_stats(stats_arrived, order, narrow, slots // wide, blocks)
    stats_parts = [stats_sends[0]] + [
        swapped(stats_sends[k], "narrow", k) for k in range(1, narrow)
    ]
    modal = place(parts)
    metric, work = place_stats(stats_parts)
    return modal, metric, work.reshape(-1)


def solution(mesh):
    return jax.shard_map(
        per_device,
        mesh=mesh,
        in_specs=(
            P(None, ("wide", "narrow")),
            P(None, ("wide", "narrow")),
            P(("wide", "narrow"), None, None),
            P(),
            P(("wide", "narrow")),
            P(("wide", "narrow")),
        ),
        out_specs=(P(None, ("wide", "narrow")), P(None, ("wide", "narrow")), P(("wide", "narrow"))),
        check_vma=False,
    )
```

```python
import jax
import jax.numpy as jnp
from jax import lax
from jax.experimental import pallas as pl
from jax.experimental.pallas import tpu as pltpu
from jax.sharding import PartitionSpec as P

f32 = jnp.float32
bf16 = jnp.bfloat16
LANES = 128
FACES = 4
AHEAD = 4
THIRD = 32

SMEM = pl.BlockSpec(memory_space=pltpu.SMEM)
VMEM = pl.BlockSpec(memory_space=pltpu.VMEM)
HBM = pl.BlockSpec(memory_space=pltpu.HBM)


def grant(*shapes):
    return pltpu.CompilerParams(vmem_limit_bytes=sum(shapes) + (1 << 20))


def far_pairs(value, axis):
    count = lax.axis_size(axis)
    return lax.ppermute(
        value, axis, [(at, (at + (1 if at % 2 else -1)) % count) for at in range(count)]
    )


def swapped(value, axis, flip):
    count = lax.axis_size(axis)
    return lax.ppermute(value, axis, [(source, source ^ flip) for source in range(count)])


def padded_rows(rows):
    return (rows // 8 + 1) * 8


def split(value, size):
    if size & (size - 1) == 0:
        return value >> (size.bit_length() - 1), value & (size - 1)
    return lax.div(value, size), lax.rem(value, size)


class Counters:
    def __init__(self, labels, largest, memory):
        self.packed = labels * 4 <= 32 and largest < 8
        self.counts = jnp.int32(0)
        self.memory = memory
        if not self.packed:

            def clear(w, _):
                memory[w] = 0
                return 0

            lax.fori_loop(0, labels, clear, 0)

    def next(self, label):
        if self.packed:
            seen = (self.counts >> (4 * label)) & 15
            self.counts = self.counts + (jnp.int32(1) << (4 * label))
        else:
            seen = self.memory[label]
            self.memory[label] = seen + 1
        return seen


def sides():
    odd_wide = lax.axis_index("wide") & 1
    odd_narrow = lax.axis_index("narrow") & 1
    return odd_wide, 1 - odd_wide, 2 + odd_narrow, 3 - odd_narrow


def halo_kernel(coef, listed, *refs):
    *outs, held, halo_blocks, sems = refs
    copies = [
        pltpu.make_async_copy(listed, halo_blocks, sems.at[0]),
        pltpu.make_async_copy(coef, held, sems.at[1]),
    ]
    for copy in copies:
        copy.start()
    for copy in copies:
        copy.wait()
    for k, side in enumerate(sides()):
        for h in range(outs[k].shape[0]):
            at = pl.multiple_of(halo_blocks[h, side] * LANES, LANES)
            outs[k][h] = held[:, pl.ds(at, LANES)]


def halo_pack(coef, halo_blocks):
    rows, elems = coef.shape
    count = halo_blocks.shape[0]
    return pl.pallas_call(
        halo_kernel,
        out_shape=[jax.ShapeDtypeStruct((count, rows, LANES), bf16)] * 4
        + [jax.ShapeDtypeStruct((rows, elems), bf16)],
        in_specs=[HBM, HBM],
        out_specs=[VMEM] * 5,
        scratch_shapes=[
            pltpu.SMEM(halo_blocks.shape, jnp.int32),
            pltpu.SemaphoreType.DMA((2,)),
        ],
        cost_estimate=pl.CostEstimate(
            flops=0, bytes_accessed=4 * rows * elems, transcendentals=0
        ),
        compiler_params=grant(4 * padded_rows(rows) * (elems + 4 * count * LANES)),
        name="halo_pack",
    )(
        pltpu.with_memory_space_constraint(coef, pltpu.HBM),
        pltpu.with_memory_space_constraint(halo_blocks, pltpu.HBM),
    )


def stats_place(w, rank, per_wide, slots):
    away = (w ^ lax.axis_index("wide")) & 1
    return away * (slots // 2) + (w >> 1) * per_wide + rank


def pack_kernel(wide, narrow, coef, owner, count, packed, route, filled):
    rows = coef.shape[0]
    slots, tall = packed.shape[0], packed.shape[1]
    blocks = owner.shape[0]
    per_wide = slots // wide

    if slots > blocks:
        for t in range(slots):
            packed[t, rows:tall, :] = jnp.full((tall - rows, LANES), -1, bf16)
    counters = Counters(wide, per_wide, filled)
    for b in range(blocks):
        w, target = split(owner[b], narrow)
        rank = counters.next(w)
        t = w * per_wide + rank
        route[0, b] = stats_place(w, rank, per_wide, slots) if slots == blocks else t
        route[1, b] = count[b]
        packed[t, 0:rows, :] = coef[:, b * LANES : (b + 1) * LANES]
        packed[t, rows:tall, :] = jnp.full((tall - rows, LANES), target.astype(f32)).astype(bf16)


def pack(coef, owner, count, wide, narrow):
    rows, elems = coef.shape
    blocks = owner.shape[0]
    slots = wide * max(1, blocks // wide)
    return pl.pallas_call(
        lambda *refs: pack_kernel(wide, narrow, *refs),
        out_shape=[
            jax.ShapeDtypeStruct((slots, padded_rows(rows), LANES), bf16),
            jax.ShapeDtypeStruct((2, blocks), jnp.int32),
        ],
        in_specs=[VMEM, SMEM, SMEM],
        out_specs=[VMEM, SMEM],
        scratch_shapes=[pltpu.SMEM((wide,), jnp.int32)],
        cost_estimate=pl.CostEstimate(flops=0, bytes_accessed=4 * rows * elems, transcendentals=0),
        compiler_params=grant(2 * rows * elems, 3 * slots * padded_rows(rows) * LANES),
        name="pack",
    )(coef, owner, count)


def metric_kernel(nb, routes, coef, h0, h1, h2, h3, w, *refs):
    *outs, table, accs, wp, idx, sem, stats, route, arrived = refs
    rows, depth = w.shape[1], w.shape[2]
    third = rows // 3
    elems = coef.shape[1]
    groups = elems // (AHEAD * LANES)

    def fetch(g, s):
        at = pl.multiple_of(g * (AHEAD * LANES), LANES)
        return pltpu.make_async_copy(nb.at[:, pl.ds(at, AHEAD * LANES)], idx.at[s], sem.at[s])

    fetch(0, 0).start()
    fetch(1, 1).start()
    routing = pltpu.make_async_copy(routes, route, arrived)
    routing.start()
    line = lax.broadcasted_iota(jnp.int32, (3 * THIRD, rows), 0)
    row = lax.broadcasted_iota(jnp.int32, (3 * THIRD, rows), 1)
    order = ((row == 3 * (line % THIRD) + line // THIRD) & (line % THIRD < third)).astype(bf16)
    spare = jnp.zeros((3 * THIRD, LANES - depth), bf16)
    for f in range(FACES + 1):
        ordered = jnp.dot(order, w[f], preferred_element_type=f32).astype(bf16)
        wp[:, f * LANES : (f + 1) * LANES] = jnp.concatenate([ordered, spare], axis=1)

    def by_element(cols):
        turned = cols.astype(f32).T
        return jnp.concatenate([turned, jnp.zeros((turned.shape[0], LANES - depth), f32)], axis=1)

    step = 512

    def fill(i, _):
        at = pl.multiple_of(i * step, step)
        table[pl.ds(at, step), :] = by_element(coef[:, pl.ds(at, step)])
        return 0

    lax.fori_loop(0, elems // step, fill, 0)
    for side, halo in zip(sides(), (h0, h1, h2, h3)):
        for h in range(halo.shape[0]):
            at = pl.multiple_of(elems + (side * halo.shape[0] + h) * LANES, LANES)
            table[pl.ds(at, LANES), :] = by_element(halo[h])

    def gather(s, p):
        for e in range(LANES):
            for f in range(FACES):
                accs[s * AHEAD + p, pl.ds(e, 1), f * LANES : (f + 1) * LANES] = table[
                    pl.ds(idx[s, f, p * LANES + e], 1), :
                ]

    def metric(b, s, p):
        at = pl.multiple_of(b * LANES, LANES)
        d = jnp.dot(
            wp[:, 0:depth], coef[:, pl.ds(at, LANES)], preferred_element_type=f32
        ) + lax.dot_general(
            wp[:, LANES:],
            accs[s * AHEAD + p].astype(bf16),
            (((1,), (1,)), ((), ())),
            preferred_element_type=f32,
        )
        x, y, z = d[0:THIRD], d[THIRD : 2 * THIRD], d[2 * THIRD :]
        inverse = 1.0 / third

        def mean(p):
            return inverse * jnp.sum(p, axis=0, keepdims=True)

        xx, yy, zz = 1.0 + mean(x * x), 1.0 + mean(y * y), 1.0 + mean(z * z)
        xy, xz, yz = mean(x * y), mean(x * z), mean(y * z)
        det = xx * (yy * zz - yz * yz) - xy * (xy * zz - yz * xz) + xz * (xy * yz - yy * xz)
        work = route[1, b].astype(f32) * jnp.sqrt(det)
        stats[route[0, b]] = jnp.concatenate([xx, yy, zz, xy, xz, yz, work, work], axis=0)

    routing.wait()

    def two_groups(i, _):
        for s in range(2):
            g = 2 * i + s
            earlier = jnp.maximum(g - 1, 0) if s == 0 else g - 1
            fetch(g, s).wait()
            for p in range(AHEAD):
                metric(earlier * AHEAD + p, 1 - s, p)
                gather(s, p)
            fetch(jnp.minimum(g + 2, groups - 1), s).start()
        return 0

    lax.fori_loop(0, groups // 2, two_groups, 0)
    for p in range(AHEAD):
        metric((groups - 1) * AHEAD + p, 1, p)
    for s in range(2):
        fetch(groups - 1, s).wait()
    size = outs[0].shape[0]
    for k, out in enumerate(outs):
        out[...] = stats[k * size : (k + 1) * size]


def metrics(nb, route, coef, halos, w, slots):
    elems = coef.shape[1]
    table = elems + sum(h.shape[0] for h in halos) * LANES
    parts = 2 if slots == elems // LANES else 1
    return pl.pallas_call(
        metric_kernel,
        out_shape=[jax.ShapeDtypeStruct((slots // parts, 8, LANES), f32)] * parts,
        in_specs=[HBM, HBM] + [VMEM] * 6,
        out_specs=[VMEM] * parts,
        scratch_shapes=[
            pltpu.VMEM((table, LANES), f32),
            pltpu.VMEM((2 * AHEAD, LANES, FACES * LANES), f32),
            pltpu.VMEM((3 * THIRD, (FACES + 1) * LANES), bf16),
            pltpu.SMEM((2, FACES, AHEAD * LANES), jnp.int32),
            pltpu.SemaphoreType.DMA((2,)),
            pltpu.VMEM((slots, 8, LANES), f32),
            pltpu.SMEM(route.shape, jnp.int32),
            pltpu.SemaphoreType.DMA(()),
        ],
        cost_estimate=pl.CostEstimate(
            flops=2 * elems * 5 * LANES * LANES, bytes_accessed=20 * elems * LANES, transcendentals=elems
        ),
        compiler_params=grant(4 * table * LANES, 3 * 104 * elems, 96 * slots * LANES, 5 << 20),
        name="metric",
    )(nb, route, coef, *halos, w)


def relay_kernel(narrow, arrived, *refs):
    sends, order, words, tags, filled, sem = refs[:narrow], *refs[narrow:]
    slots, tall = arrived.shape[0], arrived.shape[1]
    per, rows = sends[0].shape[0], sends[0].shape[1]
    for t in range(slots):
        words[t : t + 1, :] = arrived[t, tall - 8 : tall, :].astype(f32)[7:8].astype(jnp.int32)
    copy = pltpu.make_async_copy(words, tags, sem)
    copy.start()
    copy.wait()
    blocks = narrow * per
    if slots == blocks and per <= 8:
        counts = jnp.int32(0)
        for t in range(slots):
            c = tags[t, 0]
            order[c * per + ((counts >> (4 * c)) & 15)] = t
            counts = counts + (jnp.int32(1) << (4 * c))
    else:
        for c in range(narrow + 1):
            filled[c] = c * per
        for t in range(slots):
            tag = tags[t, 0]
            c = jnp.where(tag < 0, narrow, tag)
            at = filled[c]
            order[at] = t
            filled[c] = at + 1
    mine = lax.axis_index("narrow")
    for k in range(narrow):
        for j in range(per):
            sends[k][j] = arrived[order[(mine ^ k) * per + j], 0:rows, :]


def relay(arrived, rows, narrow, blocks):
    slots = arrived.shape[0]
    per = blocks // narrow
    *sends, order = pl.pallas_call(
        lambda *refs: relay_kernel(narrow, *refs),
        out_shape=[jax.ShapeDtypeStruct((per, rows, LANES), bf16)] * narrow
        + [jax.ShapeDtypeStruct((blocks + slots,), jnp.int32)],
        in_specs=[VMEM],
        out_specs=[VMEM] * narrow + [SMEM],
        scratch_shapes=[
            pltpu.VMEM((slots, LANES), jnp.int32),
            pltpu.SMEM((slots, LANES), jnp.int32),
            pltpu.SMEM((narrow + 1,), jnp.int32),
            pltpu.SemaphoreType.DMA(()),
        ],
        cost_estimate=pl.CostEstimate(
            flops=0, bytes_accessed=4 * blocks * rows * LANES, transcendentals=0
        ),
        compiler_params=grant(3 * (slots + blocks) * padded_rows(rows) * LANES),
        name="relay",
    )(arrived)
    return sends, order


def merge_kernel(kept, got, *sends):
    per = sends[0].shape[0] // 2
    mine = lax.axis_index("wide") >> 1
    for j, send in enumerate(sends):
        at = (mine ^ j) * per
        for i in range(per):
            send[i] = kept[at + i]
            send[per + i] = got[at + i]


def merge(kept, got, wide):
    half = kept.shape[0]
    groups = wide // 2
    return pl.pallas_call(
        merge_kernel,
        out_shape=[jax.ShapeDtypeStruct((2 * half // groups, 8, LANES), f32)] * groups,
        in_specs=[VMEM] * 2,
        out_specs=[VMEM] * groups,
        cost_estimate=pl.CostEstimate(flops=0, bytes_accessed=128 * half * LANES, transcendentals=0),
        compiler_params=grant(4 * 64 * half * LANES),
        name="merge",
    )(kept, got)


def relay_stats_kernel(narrow, per_wide, *refs):
    parts, order, sends, held = refs[: -narrow - 2], refs[-narrow - 2], refs[-narrow - 1 : -1], refs[-1]
    per = sends[0].shape[0]
    mine = lax.axis_index("narrow")
    wide = lax.axis_index("wide")
    size = parts[0].shape[0]
    for j, part in enumerate(parts):
        held[j * size : (j + 1) * size] = part[...]
    for k in range(narrow):
        for j in range(per):
            t = order[(mine ^ k) * per + j]
            if len(parts) > 1:
                at, rank = split(t, per_wide)
                t = (at ^ wide) * per_wide + rank
            sends[k][j] = held[t]


def relay_stats(parts, order, narrow, per_wide, blocks):
    per = blocks // narrow
    slots = len(parts) * parts[0].shape[0]
    return pl.pallas_call(
        lambda *refs: relay_stats_kernel(narrow, per_wide, *refs),
        out_shape=[jax.ShapeDtypeStruct((per, 8, LANES), f32)] * narrow,
        in_specs=[VMEM] * len(parts) + [SMEM],
        out_specs=[VMEM] * narrow,
        scratch_shapes=[pltpu.VMEM((slots, 8, LANES), f32)],
        cost_estimate=pl.CostEstimate(flops=0, bytes_accessed=64 * slots * LANES, transcendentals=0),
        compiler_params=grant(4 * 32 * (slots + blocks) * LANES),
        name="relay_stats",
    )(*parts, order)


def place_kernel(*refs):
    parts, out = refs[:-1], refs[-1]
    per = parts[0].shape[0]
    mine = lax.axis_index("narrow")
    for k, part in enumerate(parts):
        for j in range(per):
            at = pl.multiple_of(((mine ^ k) * per + j) * LANES, LANES)
            out[:, pl.ds(at, LANES)] = part[j]


def place(parts):
    per, rows, _ = parts[0].shape
    return pl.pallas_call(
        place_kernel,
        out_shape=jax.ShapeDtypeStruct((rows, len(parts) * per * LANES), bf16),
        in_specs=[VMEM] * len(parts),
        out_specs=VMEM,
        compiler_params=grant(6 * len(parts) * per * padded_rows(rows) * LANES),
        name="place",
    )(*parts)


def place_stats_kernel(*refs):
    parts, metric, work = refs[:-2], refs[-2], refs[-1]
    per = parts[0].shape[0]
    mine = lax.axis_index("narrow")
    for k, part in enumerate(parts):
        for j in range(per):
            t = (mine ^ k) * per + j
            at = pl.multiple_of(t * LANES, LANES)
            metric[:, pl.ds(at, LANES)] = part[j, 0:6, :]
            work[pl.ds(t, 1), :] = part[j, 6:7, :]


def place_stats(parts):
    per = parts[0].shape[0]
    blocks = len(parts) * per
    return pl.pallas_call(
        place_stats_kernel,
        out_shape=[
            jax.ShapeDtypeStruct((6, blocks * LANES), f32),
            jax.ShapeDtypeStruct((blocks, LANES), f32),
        ],
        in_specs=[VMEM] * len(parts),
        out_specs=[VMEM] * 2,
        compiler_params=grant(3 * 32 * blocks * LANES),
        name="place_stats",
    )(*parts)


def per_device(coefficients, neighbours, halo_blocks, recon_weight, owner_device, work_count):
    wide = lax.axis_size("wide")
    narrow = lax.axis_size("narrow")
    rows, _ = coefficients.shape
    blocks = owner_device.shape[0]
    *sent, held = halo_pack(coefficients, halo_blocks[0].T)
    halos = [
        far_pairs(sent[0], "wide"),
        swapped(sent[1], "wide", 1),
        far_pairs(sent[2], "narrow"),
        swapped(sent[3], "narrow", 1),
    ]
    packed, route = pack(held, owner_device, work_count, wide, narrow)
    slots = packed.shape[0]
    arrived = lax.all_to_all(packed, "wide", 0, 0, tiled=True)
    stats = metrics(neighbours, route, held, halos, recon_weight, slots)
    if len(stats) == 1:
        stats_arrived = [lax.all_to_all(stats[0], "wide", 0, 0, tiled=True)]
    else:
        got = swapped(stats[1], "wide", 1)
        stats_arrived = list(merge(stats[0], got, wide))
        for j in range(1, wide // 2):
            stats_arrived[j] = swapped(stats_arrived[j], "wide", 2 * j)
    sends, order = relay(arrived, rows, narrow, blocks)
    parts = [sends[0]] + [swapped(sends[k], "narrow", k) for k in range(1, narrow)]
    stats_sends = relay_stats(stats_arrived, order, narrow, slots // wide, blocks)
    stats_parts = [stats_sends[0]] + [
        swapped(stats_sends[k], "narrow", k) for k in range(1, narrow)
    ]
    modal = place(parts)
    metric, work = place_stats(stats_parts)
    return modal, metric, work.reshape(-1)


def solution(mesh):
    return jax.shard_map(
        per_device,
        mesh=mesh,
        in_specs=(
            P(None, ("wide", "narrow")),
            P(None, ("wide", "narrow")),
            P(("wide", "narrow"), None, None),
            P(),
            P(("wide", "narrow")),
            P(("wide", "narrow")),
        ),
        out_specs=(P(None, ("wide", "narrow")), P(None, ("wide", "narrow")), P(("wide", "narrow"))),
        check_vma=False,
    )
```

```python
import jax
import jax.numpy as jnp
from jax import lax
from jax.experimental import pallas as pl
from jax.experimental.pallas import tpu as pltpu
from jax.sharding import PartitionSpec as P

f32 = jnp.float32
bf16 = jnp.bfloat16
LANES = 128
FACES = 4
AHEAD = 4
THIRD = 32

SMEM = pl.BlockSpec(memory_space=pltpu.SMEM)
VMEM = pl.BlockSpec(memory_space=pltpu.VMEM)
HBM = pl.BlockSpec(memory_space=pltpu.HBM)


def grant(*shapes):
    return pltpu.CompilerParams(vmem_limit_bytes=sum(shapes) + (1 << 20))


def far_pairs(value, axis):
    count = lax.axis_size(axis)
    return lax.ppermute(
        value, axis, [(at, (at + (1 if at % 2 else -1)) % count) for at in range(count)]
    )


def swapped(value, axis, flip):
    count = lax.axis_size(axis)
    return lax.ppermute(value, axis, [(source, source ^ flip) for source in range(count)])


def padded_rows(rows):
    return (rows // 8 + 1) * 8


def split(value, size):
    if size & (size - 1) == 0:
        return value >> (size.bit_length() - 1), value & (size - 1)
    return lax.div(value, size), lax.rem(value, size)


class Counters:
    def __init__(self, labels, largest, memory):
        self.packed = labels * 4 <= 32 and largest < 8
        self.counts = jnp.int32(0)
        self.memory = memory
        if not self.packed:

            def clear(w, _):
                memory[w] = 0
                return 0

            lax.fori_loop(0, labels, clear, 0)

    def next(self, label):
        if self.packed:
            seen = (self.counts >> (4 * label)) & 15
            self.counts = self.counts + (jnp.int32(1) << (4 * label))
        else:
            seen = self.memory[label]
            self.memory[label] = seen + 1
        return seen


def sides():
    odd_wide = lax.axis_index("wide") & 1
    odd_narrow = lax.axis_index("narrow") & 1
    return odd_wide, 1 - odd_wide, 2 + odd_narrow, 3 - odd_narrow


def halo_kernel(coef, listed, *refs):
    *outs, held, halo_blocks, sems = refs
    copies = [
        pltpu.make_async_copy(listed, halo_blocks, sems.at[0]),
        pltpu.make_async_copy(coef, held, sems.at[1]),
    ]
    for copy in copies:
        copy.start()
    for copy in copies:
        copy.wait()
    for k, side in enumerate(sides()):
        for h in range(outs[k].shape[0]):
            at = pl.multiple_of(halo_blocks[h, side] * LANES, LANES)
            outs[k][h] = held[:, pl.ds(at, LANES)]


def halo_pack(coef, halo_blocks):
    rows, elems = coef.shape
    count = halo_blocks.shape[0]
    return pl.pallas_call(
        halo_kernel,
        out_shape=[jax.ShapeDtypeStruct((count, rows, LANES), bf16)] * 4
        + [jax.ShapeDtypeStruct((rows, elems), bf16)],
        in_specs=[HBM, HBM],
        out_specs=[VMEM] * 5,
        scratch_shapes=[
            pltpu.SMEM(halo_blocks.shape, jnp.int32),
            pltpu.SemaphoreType.DMA((2,)),
        ],
        cost_estimate=pl.CostEstimate(
            flops=0, bytes_accessed=4 * rows * elems, transcendentals=0
        ),
        compiler_params=grant(4 * padded_rows(rows) * (elems + 4 * count * LANES)),
        name="halo_pack",
    )(
        pltpu.with_memory_space_constraint(coef, pltpu.HBM),
        pltpu.with_memory_space_constraint(halo_blocks, pltpu.HBM),
    )


def stats_place(w, rank, per_wide, slots):
    away = (w ^ lax.axis_index("wide")) & 1
    return away * (slots // 2) + (w >> 1) * per_wide + rank


def pack_kernel(wide, narrow, coef, owner, count, packed, route, filled):
    rows = coef.shape[0]
    slots, tall = packed.shape[0], packed.shape[1]
    blocks = owner.shape[0]
    per_wide = slots // wide

    if slots > blocks:
        for t in range(slots):
            packed[t, rows:tall, :] = jnp.full((tall - rows, LANES), -1, bf16)
    counters = Counters(wide, per_wide, filled)
    for b in range(blocks):
        w, target = split(owner[b], narrow)
        rank = counters.next(w)
        t = w * per_wide + rank
        route[0, b] = stats_place(w, rank, per_wide, slots) if slots == blocks else t
        route[1, b] = count[b]
        packed[t, 0:rows, :] = coef[:, b * LANES : (b + 1) * LANES]
        packed[t, rows:tall, :] = jnp.full((tall - rows, LANES), target.astype(f32)).astype(bf16)


def pack(coef, owner, count, wide, narrow):
    rows, elems = coef.shape
    blocks = owner.shape[0]
    slots = wide * max(1, blocks // wide)
    return pl.pallas_call(
        lambda *refs: pack_kernel(wide, narrow, *refs),
        out_shape=[
            jax.ShapeDtypeStruct((slots, padded_rows(rows), LANES), bf16),
            jax.ShapeDtypeStruct((2, blocks), jnp.int32),
        ],
        in_specs=[VMEM, SMEM, SMEM],
        out_specs=[VMEM, SMEM],
        scratch_shapes=[pltpu.SMEM((wide,), jnp.int32)],
        cost_estimate=pl.CostEstimate(flops=0, bytes_accessed=4 * rows * elems, transcendentals=0),
        compiler_params=grant(2 * rows * elems, 3 * slots * padded_rows(rows) * LANES),
        name="pack",
    )(coef, owner, count)


def metric_kernel(nb, routes, coef, h0, h1, h2, h3, w, *refs):
    *outs, table, accs, wp, idx, sem, stats, route, arrived = refs
    rows, depth = w.shape[1], w.shape[2]
    third = rows // 3
    elems = coef.shape[1]
    groups = elems // (AHEAD * LANES)

    def fetch(g, s):
        at = pl.multiple_of(g * (AHEAD * LANES), LANES)
        return pltpu.make_async_copy(nb.at[:, pl.ds(at, AHEAD * LANES)], idx.at[s], sem.at[s])

    fetch(0, 0).start()
    fetch(1, 1).start()
    routing = pltpu.make_async_copy(routes, route, arrived)
    routing.start()
    line = lax.broadcasted_iota(jnp.int32, (3 * THIRD, rows), 0)
    row = lax.broadcasted_iota(jnp.int32, (3 * THIRD, rows), 1)
    order = ((row == 3 * (line % THIRD) + line // THIRD) & (line % THIRD < third)).astype(bf16)
    spare = jnp.zeros((3 * THIRD, LANES - depth), bf16)
    for f in range(FACES + 1):
        ordered = jnp.dot(order, w[f], preferred_element_type=f32).astype(bf16)
        wp[:, f * LANES : (f + 1) * LANES] = jnp.concatenate([ordered, spare], axis=1)

    def by_element(cols):
        turned = cols.astype(f32).T
        return jnp.concatenate([turned, jnp.zeros((turned.shape[0], LANES - depth), f32)], axis=1)

    step = 512

    def fill(i, _):
        at = pl.multiple_of(i * step, step)
        table[pl.ds(at, step), :] = by_element(coef[:, pl.ds(at, step)])
        return 0

    lax.fori_loop(0, elems // step, fill, 0)
    for side, halo in zip(sides(), (h0, h1, h2, h3)):
        for h in range(halo.shape[0]):
            at = pl.multiple_of(elems + (side * halo.shape[0] + h) * LANES, LANES)
            table[pl.ds(at, LANES), :] = by_element(halo[h])

    def gather(s, p):
        for e in range(LANES):
            for f in range(FACES):
                accs[s * AHEAD + p, pl.ds(e, 1), f * LANES : (f + 1) * LANES] = table[
                    pl.ds(idx[s, f, p * LANES + e], 1), :
                ]

    def metric(b, s, p):
        at = pl.multiple_of(b * LANES, LANES)
        d = jnp.dot(
            wp[:, 0:depth], coef[:, pl.ds(at, LANES)], preferred_element_type=f32
        ) + lax.dot_general(
            wp[:, LANES:],
            accs[s * AHEAD + p].astype(bf16),
            (((1,), (1,)), ((), ())),
            preferred_element_type=f32,
        )
        x, y, z = d[0:THIRD], d[THIRD : 2 * THIRD], d[2 * THIRD :]
        inverse = 1.0 / third

        def mean(p):
            return inverse * jnp.sum(p, axis=0, keepdims=True)

        xx, yy, zz = 1.0 + mean(x * x), 1.0 + mean(y * y), 1.0 + mean(z * z)
        xy, xz, yz = mean(x * y), mean(x * z), mean(y * z)
        det = xx * (yy * zz - yz * yz) - xy * (xy * zz - yz * xz) + xz * (xy * yz - yy * xz)
        work = route[1, b].astype(f32) * jnp.sqrt(det)
        stats[route[0, b]] = jnp.concatenate([xx, yy, zz, xy, xz, yz, work, work], axis=0)

    routing.wait()

    def two_groups(i, _):
        for s in range(2):
            g = 2 * i + s
            earlier = jnp.maximum(g - 1, 0) if s == 0 else g - 1
            fetch(g, s).wait()
            for p in range(AHEAD):
                metric(earlier * AHEAD + p, 1 - s, p)
                gather(s, p)
            fetch(jnp.minimum(g + 2, groups - 1), s).start()
        return 0

    lax.fori_loop(0, groups // 2, two_groups, 0)
    for p in range(AHEAD):
        metric((groups - 1) * AHEAD + p, 1, p)
    for s in range(2):
        fetch(groups - 1, s).wait()
    size = outs[0].shape[0]
    for k, out in enumerate(outs):
        out[...] = stats[k * size : (k + 1) * size]


def metrics(nb, route, coef, halos, w, slots):
    elems = coef.shape[1]
    table = elems + sum(h.shape[0] for h in halos) * LANES
    parts = 2 if slots == elems // LANES else 1
    return pl.pallas_call(
        metric_kernel,
        out_shape=[jax.ShapeDtypeStruct((slots // parts, 8, LANES), f32)] * parts,
        in_specs=[HBM, HBM] + [VMEM] * 6,
        out_specs=[VMEM] * parts,
        scratch_shapes=[
            pltpu.VMEM((table, LANES), f32),
            pltpu.VMEM((2 * AHEAD, LANES, FACES * LANES), f32),
            pltpu.VMEM((3 * THIRD, (FACES + 1) * LANES), bf16),
            pltpu.SMEM((2, FACES, AHEAD * LANES), jnp.int32),
            pltpu.SemaphoreType.DMA((2,)),
            pltpu.VMEM((slots, 8, LANES), f32),
            pltpu.SMEM(route.shape, jnp.int32),
            pltpu.SemaphoreType.DMA(()),
        ],
        cost_estimate=pl.CostEstimate(
            flops=2 * elems * 5 * LANES * LANES, bytes_accessed=20 * elems * LANES, transcendentals=elems
        ),
        compiler_params=grant(4 * table * LANES, 3 * 104 * elems, 96 * slots * LANES, 5 << 20),
        name="metric",
    )(nb, route, coef, *halos, w)


def relay_kernel(narrow, arrived, *refs):
    sends, order, words, tags, filled, sem = refs[:narrow], *refs[narrow:]
    slots, tall = arrived.shape[0], arrived.shape[1]
    per, rows = sends[0].shape[0], sends[0].shape[1]
    for t in range(slots):
        words[t : t + 1, :] = arrived[t, tall - 8 : tall, :].astype(f32)[7:8].astype(jnp.int32)
    copy = pltpu.make_async_copy(words, tags, sem)
    copy.start()
    copy.wait()
    blocks = narrow * per
    if slots == blocks and per <= 8:
        counts = jnp.int32(0)
        for t in range(slots):
            c = tags[t, 0]
            order[c * per + ((counts >> (4 * c)) & 15)] = t
            counts = counts + (jnp.int32(1) << (4 * c))
    else:
        for c in range(narrow + 1):
            filled[c] = c * per
        for t in range(slots):
            tag = tags[t, 0]
            c = jnp.where(tag < 0, narrow, tag)
            at = filled[c]
            order[at] = t
            filled[c] = at + 1
    mine = lax.axis_index("narrow")
    for k in range(narrow):
        for j in range(per):
            sends[k][j] = arrived[order[(mine ^ k) * per + j], 0:rows, :]


def relay(arrived, rows, narrow, blocks):
    slots = arrived.shape[0]
    per = blocks // narrow
    *sends, order = pl.pallas_call(
        lambda *refs: relay_kernel(narrow, *refs),
        out_shape=[jax.ShapeDtypeStruct((per, rows, LANES), bf16)] * narrow
        + [jax.ShapeDtypeStruct((blocks + slots,), jnp.int32)],
        in_specs=[VMEM],
        out_specs=[VMEM] * narrow + [SMEM],
        scratch_shapes=[
            pltpu.VMEM((slots, LANES), jnp.int32),
            pltpu.SMEM((slots, LANES), jnp.int32),
            pltpu.SMEM((narrow + 1,), jnp.int32),
            pltpu.SemaphoreType.DMA(()),
        ],
        cost_estimate=pl.CostEstimate(
            flops=0, bytes_accessed=4 * blocks * rows * LANES, transcendentals=0
        ),
        compiler_params=grant(3 * (slots + blocks) * padded_rows(rows) * LANES),
        name="relay",
    )(arrived)
    return sends, order


def merge_kernel(kept, got, *sends):
    per = sends[0].shape[0] // 2
    mine = lax.axis_index("wide") >> 1
    for j, send in enumerate(sends):
        at = (mine ^ j) * per
        for i in range(per):
            send[i] = kept[at + i]
            send[per + i] = got[at + i]


def merge(kept, got, wide):
    half = kept.shape[0]
    groups = wide // 2
    return pl.pallas_call(
        merge_kernel,
        out_shape=[jax.ShapeDtypeStruct((2 * half // groups, 8, LANES), f32)] * groups,
        in_specs=[VMEM] * 2,
        out_specs=[VMEM] * groups,
        cost_estimate=pl.CostEstimate(flops=0, bytes_accessed=128 * half * LANES, transcendentals=0),
        compiler_params=grant(4 * 64 * half * LANES),
        name="merge",
    )(kept, got)


def relay_stats_kernel(narrow, per_wide, *refs):
    parts, order, sends, held = refs[: -narrow - 2], refs[-narrow - 2], refs[-narrow - 1 : -1], refs[-1]
    per = sends[0].shape[0]
    mine = lax.axis_index("narrow")
    wide = lax.axis_index("wide")
    size = parts[0].shape[0]
    for j, part in enumerate(parts):
        held[j * size : (j + 1) * size] = part[...]
    for k in range(narrow):
        for j in range(per):
            t = order[(mine ^ k) * per + j]
            if len(parts) > 1:
                at, rank = split(t, per_wide)
                t = (at ^ wide) * per_wide + rank
            sends[k][j] = held[t]


def relay_stats(parts, order, narrow, per_wide, blocks):
    per = blocks // narrow
    slots = len(parts) * parts[0].shape[0]
    return pl.pallas_call(
        lambda *refs: relay_stats_kernel(narrow, per_wide, *refs),
        out_shape=[jax.ShapeDtypeStruct((per, 8, LANES), f32)] * narrow,
        in_specs=[VMEM] * len(parts) + [SMEM],
        out_specs=[VMEM] * narrow,
        scratch_shapes=[pltpu.VMEM((slots, 8, LANES), f32)],
        cost_estimate=pl.CostEstimate(flops=0, bytes_accessed=64 * slots * LANES, transcendentals=0),
        compiler_params=grant(4 * 32 * (slots + blocks) * LANES),
        name="relay_stats",
    )(*parts, order)


def place_kernel(flips, *refs):
    parts, out, sems = refs[: len(flips)], refs[-2], refs[-1]
    per = parts[0].shape[0]
    mine = lax.axis_index("narrow")
    copies = []
    for i, part in enumerate(parts):
        for j in range(per):
            at = pl.multiple_of(((mine ^ flips[i]) * per + j) * LANES, LANES)
            copies.append(
                pltpu.make_async_copy(part.at[j], out.at[:, pl.ds(at, LANES)], sems.at[i, j])
            )
    for copy in copies:
        copy.start()
    for copy in copies:
        copy.wait()


def place(parts, flips, total, so_far=None):
    per, rows, _ = parts[0].shape
    earlier = [] if so_far is None else [so_far]
    return pl.pallas_call(
        lambda *refs: place_kernel(flips, *refs),
        out_shape=jax.ShapeDtypeStruct((rows, total * per * LANES), bf16),
        in_specs=[VMEM] * len(parts) + [HBM] * len(earlier),
        out_specs=HBM,
        scratch_shapes=[pltpu.SemaphoreType.DMA((len(parts), per))],
        input_output_aliases={len(parts): 0} if earlier else {},
        cost_estimate=pl.CostEstimate(
            flops=0, bytes_accessed=4 * len(parts) * per * rows * LANES, transcendentals=0
        ),
        compiler_params=grant(6 * len(parts) * per * padded_rows(rows) * LANES),
    )(*parts, *earlier)


def place_stats_kernel(*refs):
    parts, metric, work = refs[:-2], refs[-2], refs[-1]
    per = parts[0].shape[0]
    mine = lax.axis_index("narrow")
    for k, part in enumerate(parts):
        for j in range(per):
            t = (mine ^ k) * per + j
            at = pl.multiple_of(t * LANES, LANES)
            metric[:, pl.ds(at, LANES)] = part[j, 0:6, :]
            work[pl.ds(t, 1), :] = part[j, 6:7, :]


def place_stats(parts):
    per = parts[0].shape[0]
    blocks = len(parts) * per
    return pl.pallas_call(
        place_stats_kernel,
        out_shape=[
            jax.ShapeDtypeStruct((6, blocks * LANES), f32),
            jax.ShapeDtypeStruct((blocks, LANES), f32),
        ],
        in_specs=[VMEM] * len(parts),
        out_specs=[VMEM] * 2,
        compiler_params=grant(3 * 32 * blocks * LANES),
        name="place_stats",
    )(*parts)


def per_device(coefficients, neighbours, halo_blocks, recon_weight, owner_device, work_count):
    wide = lax.axis_size("wide")
    narrow = lax.axis_size("narrow")
    rows, _ = coefficients.shape
    blocks = owner_device.shape[0]
    *sent, held = halo_pack(coefficients, halo_blocks[0].T)
    halos = [
        far_pairs(sent[0], "wide"),
        swapped(sent[1], "wide", 1),
        far_pairs(sent[2], "narrow"),
        swapped(sent[3], "narrow", 1),
    ]
    packed, route = pack(held, owner_device, work_count, wide, narrow)
    slots = packed.shape[0]
    arrived = lax.all_to_all(packed, "wide", 0, 0, tiled=True)
    stats = metrics(neighbours, route, held, halos, recon_weight, slots)
    if len(stats) == 1:
        stats_arrived = [lax.all_to_all(stats[0], "wide", 0, 0, tiled=True)]
    else:
        got = swapped(stats[1], "wide", 1)
        stats_arrived = list(merge(stats[0], got, wide))
        for j in range(1, wide // 2):
            stats_arrived[j] = swapped(stats_arrived[j], "wide", 2 * j)
    sends, order = relay(arrived, rows, narrow, blocks)
    parts = [sends[0]] + [swapped(sends[k], "narrow", k) for k in range(1, narrow)]
    stats_sends = relay_stats(stats_arrived, order, narrow, slots // wide, blocks)
    stats_parts = [stats_sends[0]] + [
        swapped(stats_sends[k], "narrow", k) for k in range(1, narrow)
    ]
    modal = place(parts[:2], (0, 1), narrow)
    modal = place(parts[2:], tuple(range(2, narrow)), narrow, modal)
    metric, work = place_stats(stats_parts)
    return modal, metric, work.reshape(-1)


def solution(mesh):
    return jax.shard_map(
        per_device,
        mesh=mesh,
        in_specs=(
            P(None, ("wide", "narrow")),
            P(None, ("wide", "narrow")),
            P(("wide", "narrow"), None, None),
            P(),
            P(("wide", "narrow")),
            P(("wide", "narrow")),
        ),
        out_specs=(P(None, ("wide", "narrow")), P(None, ("wide", "narrow")), P(("wide", "narrow"))),
        check_vma=False,
    )
```
